32 devices in a mesh: groups: 2 (over y), atoms: 8 (over z, x), waves: 2 (over core).
Axes of the slice: x: 2, y: 2, z: 4, core: 2. Of those that a mesh axis runs over, the one named last changes fastest.
Arguments:
- features: bfloat16 [8192, 256], P(('groups', 'atoms', 'waves')), parts along dimension 0, may hold values from -6 to 6
- positions: float32 [3, 8192], P(None, ('groups', 'atoms', 'waves')), parts along dimension 1, may hold values from 0 to 1, as said below
- distances: float32 [8192, 768], P(('groups', 'atoms', 'waves')), parts along dimension 0, may hold values from 0.5 to 5
- pair_mask: int32 [8192, 768], P(('groups', 'atoms', 'waves')), parts along dimension 0, may hold values 0 or 1
- counts: int32 [32], P(('groups', 'atoms', 'waves')), parts along dimension 0, may hold values from 128 to 256, as said below
- wave_index: int32 [3, 2048], P(None, ('groups', 'waves')), parts along dimension 1, may hold values from -6 to 6
- w_value: bfloat16 [256, 256], replicated, may hold values from -0.375 to 0.375
- filter_short: float32 [16, 256], replicated, may hold values from -1 to 1
- filter_long: float32 [16, 256], replicated, may hold values from -6 to 6
- gain: float32 [256], replicated, may hold values from 0.1 to 1.9
- w_inner: bfloat16 [256, 256], replicated, may hold values from -0.375 to 0.375
- w_outer: bfloat16 [256, 256], replicated, may hold values from -0.375 to 0.375
Outputs:
- updated: bfloat16 [8192, 256], P(('groups', 'atoms', 'waves')), parts along dimension 0
The draws below stay inside these ranges and needn't reach their ends.
There are 2 independent parts, one for each index of `groups`. The reference program is written for one: setup_inputs(seed, part) draws one part's arguments, and reference() takes and returns one part's arrays. A program takes and returns all parts, laid end to end along the dimension named above; an argument that names none is the same for every part. Nothing has to cross between parts.
Inputs may be any that keep to these rules, and one draw needn't show every extreme that they name: The atoms of box b are its first counts[b] slots; in every draw some box is full. `positions`: fractional coordinates; the first coordinate of every slot of box b lies in [b / 16, (b + 1) / 16).
All inputs are finite; a program needn't handle non-finite values. No bound on the sum of `pair_mask` on one device may be relied on, other than what follows from the above.
Results may differ from the reference program's by a relative error of at most 0.015.
Values may be sent and summed in bfloat16 or wider, within the bound.
No kernel may reach another device: no remote copies, remote signals or barrier semaphores. Data moves between devices by JAX's collectives and lax.ppermute only.
A program may use at most 64 MiB of HBM per device.

```python
import jax
import jax.numpy as jnp
from jax import lax

F = 256
NRBF = 16
ATOM_DEV = 256
BOXES = 16
ATOMS = 4096
KWAVES = 1024


def draw_positions(key, part):
    uniform = jax.random.uniform(key, (3, ATOMS), jnp.float32)
    box_of = (jnp.arange(ATOMS, dtype=jnp.int32) // ATOM_DEV).astype(jnp.float32)
    coord_first = (box_of + uniform[0]) / BOXES
    return jnp.stack([coord_first, uniform[1], uniform[2]]).astype(jnp.float32)


def draw_counts(key, part):
    keyone, keytwo = jax.random.split(jax.random.fold_in(key, 17))
    occupancy = jax.random.randint(keyone, (BOXES,), ATOM_DEV // 2, ATOM_DEV + 1)
    fullest = jax.random.randint(keytwo, (), 0, BOXES)
    return jnp.where(jnp.arange(BOXES, dtype=jnp.int32) == fullest, ATOM_DEV, occupancy).astype(jnp.int32)


def place_ends(values, own_key, smallest, largest):
    index_at = [jax.random.randint(jax.random.fold_in(own_key, axis), (), 0, length) for axis, length in enumerate(values.shape)]
    main_axis = values.shape.index(max(values.shape))
    neighbour = index_at[:main_axis] + [(index_at[main_axis] + 1) % values.shape[main_axis]] + index_at[main_axis + 1:]
    return values.at[tuple(index_at)].set(smallest).at[tuple(neighbour)].set(largest)


def block_levels(key, dims, cuts, low, top_value):
    factor_of = 1.0
    for position, parts in cuts:
        draws = jax.random.uniform(jax.random.fold_in(jax.random.fold_in(key, 6), position), (parts,), jnp.float32, low / len(cuts), top_value / len(cuts))
        factor_of = factor_of * jnp.repeat(jnp.exp(draws), dims[position] // parts).reshape((-1,) + (1,) * (len(dims) - 1 - position))
    return factor_of


def centred(rng, dims, scale, most, pieces=(), held_as=jnp.bfloat16):
    entries = scale * jax.random.normal(rng, dims, jnp.float32)
    if pieces:
        entries = entries * block_levels(rng, dims, pieces, -0.22, 0.18)
    return jnp.clip(entries, -most, most).astype(held_as)


def setup_inputs(seed: int = 0, part: int = 0) -> dict:
    key_of = jax.random.split(jax.random.key(seed), 13)
    part_keys = jax.random.split(jax.random.fold_in(key_of[12], part), 13)
    features = centred(part_keys[0], (ATOMS, F), 1.0, 6.0, ((0, 16),))
    positions = draw_positions(jax.random.fold_in(jax.random.fold_in(key_of[12], part), 71), part)
    distances = jnp.clip(0.5 + 4.5 * jax.random.uniform(part_keys[2], (ATOMS, 3 * ATOM_DEV), jnp.float32) ** block_levels(part_keys[2], (ATOMS, 3 * ATOM_DEV), ((0, 16),), -0.2, 0.2), 0.5, 5.0)
    pair_mask = place_ends((jax.random.randint(part_keys[3], (ATOMS, 3 * ATOM_DEV), 0, 2) < 1).astype(jnp.int32), jax.random.fold_in(part_keys[3], 1), 0, 1)
    counts = draw_counts(jax.random.fold_in(jax.random.fold_in(key_of[12], part), 71), part)
    wave_index = place_ends(jax.random.randint(part_keys[5], (3, KWAVES), -6, 7), jax.random.fold_in(part_keys[5], 1), -6, 6).astype(jnp.int32)
    w_value = centred(key_of[6], (F, F), F ** -0.5, 0.375)
    filter_short = centred(key_of[7], (NRBF, F), (ATOM_DEV ** -0.5), 1.0, (), jnp.float32)
    filter_long = centred(key_of[8], (NRBF, F), 2.0, 6.0, (), jnp.float32)
    gain = jnp.clip(1.0 + 0.18 * jax.random.normal(key_of[9], (F,), jnp.float32), 0.1, 1.9)
    w_inner = centred(key_of[10], (F, F), F ** -0.5, 0.375)
    w_outer = centred(key_of[11], (F, F), F ** -0.5, 0.375)
    return {"features": features, "positions": positions, "distances": distances, "pair_mask": pair_mask, "counts": counts, "wave_index": wave_index, "w_value": w_value, "filter_short": filter_short, "filter_long": filter_long, "gain": gain, "w_inner": w_inner, "w_outer": w_outer}


radius_cut = 5.0
wave_top = 6.0 * 3.0 ** 0.5

def radial_tiles(distances, pair_mask, radial_count):
    centres = radius_cut * jnp.arange(radial_count, dtype=jnp.float32) / (radial_count - 1)
    spacing = radius_cut / (radial_count - 1)
    envelope = 0.5 * (jnp.cos(jnp.pi * distances / radius_cut) + 1.0) * pair_mask.astype(jnp.float32)
    offsets = (distances[None] - centres[:, None, None]) / spacing
    tiles = jnp.exp(-0.5 * offsets * offsets) * envelope[None]
    return tiles.astype(jnp.bfloat16)

def phase_tiles(points, wave_index):
    waves = wave_index.astype(jnp.float32)
    theta = points[0][:, None] * waves[0][None, :] + points[1][:, None] * waves[1][None, :]
    theta = 2.0 * jnp.pi * (theta + points[2][:, None] * waves[2][None, :])
    return (jnp.cos(theta).astype(jnp.bfloat16), jnp.sin(theta).astype(jnp.bfloat16))

def wave_filter(wave_index, filter_long):
    waves = wave_index.astype(jnp.float32)
    radial_count = filter_long.shape[0]
    magnitude = jnp.sqrt(waves[0] * waves[0] + waves[1] * waves[1] + waves[2] * waves[2])
    centres = wave_top * jnp.arange(radial_count, dtype=jnp.float32) / (radial_count - 1)
    spacing = wave_top / (radial_count - 1)
    offsets = (magnitude[None, :] - centres[:, None]) / spacing
    k_basis = jnp.exp(-0.5 * offsets * offsets)
    return jnp.dot(k_basis.T, filter_long, precision=lax.Precision.HIGHEST)

def reference(features, positions, distances, pair_mask, counts, wave_index, w_value, filter_short, filter_long, gain, w_inner, w_outer):
    slot_index = jnp.arange(ATOMS, dtype=jnp.int32)
    occupied = (slot_index % ATOM_DEV < jnp.repeat(counts, ATOM_DEV)).astype(jnp.float32)
    values = (jnp.dot(features, w_value, preferred_element_type=jnp.float32) * occupied[:, None]).astype(jnp.bfloat16)
    extended = jnp.concatenate([values[ATOMS - ATOM_DEV:], values, values[:ATOM_DEV]], 0)

    def near_box(box):
        begin = (box * ATOM_DEV).astype(jnp.int32)
        beside_all = lax.dynamic_slice_in_dim(extended, begin, 3 * ATOM_DEV, 0)
        box_dist = lax.dynamic_slice_in_dim(distances, begin, ATOM_DEV, 0)
        box_mask = lax.dynamic_slice_in_dim(pair_mask, begin, ATOM_DEV, 0)
        tiles = radial_tiles(box_dist, box_mask, NRBF).reshape(NRBF * ATOM_DEV, 3 * ATOM_DEV)
        products = jnp.dot(tiles.astype(jnp.float32), beside_all.astype(jnp.float32), precision=lax.Precision.HIGHEST)
        products = products.reshape(NRBF, ATOM_DEV, F)
        return lax.optimization_barrier(jnp.sum(products * filter_short[:, None, :], axis=0))
    near_field = lax.map(near_box, jnp.arange(BOXES, dtype=jnp.int32)).reshape(ATOMS, F)
    block = 2 * ATOM_DEV
    block_ids = jnp.arange(ATOMS // block, dtype=jnp.int32)

    def add_factors(carry, index):
        begin = (index * block).astype(jnp.int32)
        points = lax.dynamic_slice_in_dim(positions, begin, block, 1)
        block_values = lax.dynamic_slice_in_dim(values, begin, block, 0)
        cosine, sine = phase_tiles(points, wave_index)
        cos_acc = carry[0] + jnp.dot(cosine.T, block_values, preferred_element_type=jnp.float32)
        sin_acc = carry[1] + jnp.dot(sine.T, block_values, preferred_element_type=jnp.float32)
        return ((cos_acc, sin_acc), None)
    zeros = jnp.zeros((KWAVES, F), jnp.float32)
    (cos_sum, sin_sum), unused = lax.scan(add_factors, (zeros, zeros), block_ids)
    filt = wave_filter(wave_index, filter_long)
    factor_scale = float(ATOMS) ** (-0.5)
    cos_filtered = (cos_sum * filt * factor_scale).astype(jnp.bfloat16)
    sin_filtered = (sin_sum * filt * factor_scale).astype(jnp.bfloat16)

    def far_block(index):
        begin = (index * block).astype(jnp.int32)
        points = lax.dynamic_slice_in_dim(positions, begin, block, 1)
        cosine, sine = phase_tiles(points, wave_index)
        summed = jnp.dot(cosine, cos_filtered, preferred_element_type=jnp.float32) + jnp.dot(sine, sin_filtered, preferred_element_type=jnp.float32)
        return summed * float(KWAVES) ** (-0.5)
    far_field = lax.map(far_block, block_ids).reshape(ATOMS, F)
    combined = features.astype(jnp.float32) + near_field + far_field
    normed = (combined * lax.rsqrt(lax.optimization_barrier(jnp.mean(combined * combined, axis=-1, keepdims=True)) + 1e-06) * gain).astype(jnp.bfloat16)
    inner = jax.nn.silu(jnp.dot(normed, w_inner, preferred_element_type=jnp.float32)).astype(jnp.bfloat16)
    result = jnp.dot(inner, w_outer, preferred_element_type=jnp.float32) * occupied[:, None]
    return result.astype(jnp.bfloat16)
```

```python
import functools
import math

import jax
import jax.numpy as jnp
from jax import lax
from jax.experimental import pallas as pl
from jax.experimental.pallas import tpu as pltpu
from jax.sharding import PartitionSpec as P

radius_cut = 5.0
wave_top = 6.0 * 3.0**0.5
both = ("atoms", "waves")
gather_limit = 8
extra_rows = 16

cos_terms = (
    0.9999992107823219,
    -19.738980355764046,
    64.92865742103481,
    -85.27162153431601,
    58.7904921202013,
    -21.071105627744192,
)
sin_terms = (
    6.283184916495436,
    -41.341589232689465,
    81.59994332980449,
    -76.61447253146167,
    41.34288235547851,
    -12.471243536446185,
)


def padded(block, sides, width):
    for axis, dim in sides:
        count = lax.axis_size(axis)
        forward = [(i, i + 1) for i in range(count - 1)]
        forward.append((count - 1, 0))
        backward = [(target, source) for source, target in forward]
        low = lax.ppermute(
            lax.slice_in_dim(block, block.shape[dim] - width, None, axis=dim), axis, forward
        )
        high = lax.ppermute(lax.slice_in_dim(block, 0, width, axis=dim), axis, backward)
        block = jnp.concatenate([low, block, high], axis=dim)
    return block


def radial_tiles(distances, pair_mask, radial_count):
    centres = radius_cut * jnp.arange(radial_count, dtype=jnp.float32) / (radial_count - 1)
    spacing = radius_cut / (radial_count - 1)
    envelope = (
        0.5 * (jnp.cos(jnp.pi * distances / radius_cut) + 1.0) * pair_mask.astype(jnp.float32)
    )
    offsets = (distances[None] - centres[:, None, None]) / spacing
    tiles = jnp.exp(-0.5 * offsets * offsets) * envelope[None]
    return tiles.astype(jnp.bfloat16)


def phase_tiles(points, wave_index):
    waves = wave_index.astype(jnp.float32)
    theta = points[0][:, None] * waves[0][None, :] + points[1][:, None] * waves[1][None, :]
    theta = 2.0 * jnp.pi * (theta + points[2][:, None] * waves[2][None, :])
    return (jnp.cos(theta).astype(jnp.bfloat16), jnp.sin(theta).astype(jnp.bfloat16))


def wave_filter(wave_index, filter_long):
    waves = wave_index.astype(jnp.float32)
    radial_count = filter_long.shape[0]
    magnitude = jnp.sqrt(waves[0] * waves[0] + waves[1] * waves[1] + waves[2] * waves[2])
    centres = wave_top * jnp.arange(radial_count, dtype=jnp.float32) / (radial_count - 1)
    spacing = wave_top / (radial_count - 1)
    offsets = (magnitude[None, :] - centres[:, None]) / spacing
    k_basis = jnp.exp(-0.5 * offsets * offsets)
    return jnp.dot(k_basis.T, filter_long, precision=lax.Precision.HIGHEST)


def summed_body(
    features,
    positions,
    distances,
    pair_mask,
    counts,
    wave_index,
    w_value,
    filter_short,
    filter_long,
    gain,
    w_inner,
    w_outer,
):
    row_count = features.shape[0]
    width = features.shape[1]
    radial_count = filter_short.shape[0]
    occupied = (lax.iota(jnp.int32, row_count) < counts[0]).astype(jnp.float32)
    values = (
        jnp.dot(features, w_value, preferred_element_type=jnp.float32) * occupied[:, None]
    ).astype(jnp.bfloat16)
    beside_all = padded(values, ((("atoms", "waves"), 0),), row_count)
    tiles = radial_tiles(distances, pair_mask, radial_count).reshape(
        radial_count * row_count, 3 * row_count
    )
    products = jnp.dot(tiles, beside_all, preferred_element_type=jnp.float32).reshape(
        radial_count, row_count, width
    )
    near_field = jnp.sum(products * filter_short[:, None, :], axis=0)
    wide_values, block_points = (
        lax.all_gather(values.astype(jnp.float32), "waves", axis=0, tiled=True),
        lax.all_gather(positions, "waves", axis=1, tiled=True),
    )
    block_values = wide_values.astype(jnp.bfloat16)
    cosine, sine = phase_tiles(block_points, wave_index)
    cos_sum = jnp.einsum("ak,af->kf", cosine, block_values, preferred_element_type=jnp.float32)
    sin_sum = jnp.einsum("ak,af->kf", sine, block_values, preferred_element_type=jnp.float32)
    atom_total = row_count * lax.axis_size(("atoms", "waves"))
    wave_total = wave_index.shape[1] * lax.axis_size("waves")
    factor_scale = float(atom_total) ** (-0.5)
    cos_total, sin_total = lax.psum((cos_sum, sin_sum), "atoms")
    block_filter = wave_filter(wave_index, filter_long)
    cos_filtered = (cos_total * block_filter * factor_scale).astype(jnp.bfloat16)
    sin_filtered = (sin_total * block_filter * factor_scale).astype(jnp.bfloat16)
    far_field = lax.psum_scatter(
        (
            jnp.dot(cosine, cos_filtered, preferred_element_type=jnp.float32)
            + jnp.dot(sine, sin_filtered, preferred_element_type=jnp.float32)
        ).astype(jnp.bfloat16),
        "waves",
        scatter_dimension=0,
        tiled=True,
    ).astype(jnp.float32) * float(wave_total) ** (-0.5)
    combined = features.astype(jnp.float32) + near_field + far_field
    normed = (
        combined * lax.rsqrt(jnp.mean(combined * combined, axis=-1, keepdims=True) + 1e-06) * gain
    ).astype(jnp.bfloat16)
    inner = jax.nn.silu(jnp.dot(normed, w_inner, preferred_element_type=jnp.float32)).astype(
        jnp.bfloat16
    )
    result = jnp.dot(inner, w_outer, preferred_element_type=jnp.float32) * occupied[:, None]
    return result.astype(jnp.bfloat16)


def horner(terms, w):
    total = jnp.full_like(w, terms[-1])
    for term in terms[-2::-1]:
        total = total * w + term
    return total


def phases(turns):
    r = turns - jnp.round(turns)
    w = r * r
    return horner(cos_terms, w), r * horner(sin_terms, w)


def fill_phases(phase_ref, column, wave_ref, point_rows, step=64):
    wave_count = wave_ref.shape[0]
    width = point_rows.shape[1]
    for low in range(0, wave_count, step):
        turns = jnp.dot(
            wave_ref[low : low + step, :], point_rows, preferred_element_type=jnp.float32
        )
        cosine, sine = phases(turns)
        phase_ref[low : low + step, column : column + width] = cosine.astype(jnp.bfloat16)
        phase_ref[wave_count + low : wave_count + low + step, column : column + width] = (
            sine.astype(jnp.bfloat16)
        )


def block_sums(phase_ref, wave_ref, first, second):
    rows = first.shape[0] - extra_rows
    fill_phases(phase_ref, 0, wave_ref, first[rows:, :])
    fill_phases(phase_ref, rows, wave_ref, second[rows:, :])
    block_values = jnp.concatenate([first[:rows, :], second[:rows, :]], axis=0)
    return jnp.dot(phase_ref[...], block_values, preferred_element_type=jnp.float32)


def prepare_kernel(count_ref, features_ref, w_value_ref, positions_ref, wave_ref, chunk_ref, waves_ref):
    rows = features_ref.shape[0]
    values = jnp.dot(features_ref[...], w_value_ref[...], preferred_element_type=jnp.float32)
    row = lax.broadcasted_iota(jnp.int32, values.shape, 0)
    chunk_ref[:rows, :] = jnp.where(row < count_ref[0], values, 0.0).astype(jnp.bfloat16)
    points = positions_ref[...]
    high = points.astype(jnp.bfloat16).astype(jnp.float32)
    middle = (points - high).astype(jnp.bfloat16).astype(jnp.float32)
    low = points - high - middle
    spare = jnp.zeros((extra_rows - 9, rows), jnp.float32)
    chunk_ref[rows:, :] = jnp.concatenate([high, middle, low, spare], axis=0).astype(jnp.bfloat16)
    waves = wave_ref[...].astype(jnp.float32)
    spare = jnp.zeros((extra_rows - 9, waves.shape[1]), jnp.float32)
    waves_ref[...] = jnp.concatenate([waves, waves, waves, spare], axis=0).T.astype(jnp.bfloat16)


def filter_kernel(scale, wave_ref, filter_long_ref, out_ref):
    waves = wave_ref[...].astype(jnp.float32)
    radial_count = filter_long_ref.shape[0]
    magnitude = jnp.sqrt(
        waves[0:1] * waves[0:1] + waves[1:2] * waves[1:2] + waves[2:3] * waves[2:3]
    )
    spacing = wave_top / (radial_count - 1)
    index = lax.broadcasted_iota(jnp.int32, (radial_count, waves.shape[1]), 0)
    offsets = magnitude / spacing - index.astype(jnp.float32)
    basis = jnp.exp(-0.5 * offsets * offsets)
    out_ref[...] = scale * jnp.dot(
        basis.T,
        filter_long_ref[...],
        precision=lax.Precision.HIGHEST,
        preferred_element_type=jnp.float32,
    )


def own_kernel(wave_ref, first_ref, second_ref, sums_ref, phase_ref):
    sums_ref[...] = block_sums(phase_ref, wave_ref, first_ref, second_ref)


def more_kernel(pairs, wave_ref, sums_in_ref, *refs):
    chunks, (sums_ref, phase_ref) = refs[: 2 * pairs], refs[2 * pairs :]
    for i in range(pairs):
        base = sums_in_ref if i == 0 else sums_ref
        sums_ref[...] = base[...] + block_sums(
            phase_ref.at[i % 2], wave_ref, chunks[2 * i], chunks[2 * i + 1]
        )


def weighted(products, rows, first, filter_ref, radial_count):
    total = None
    for i in range(products.shape[0] // rows):
        m = first + i - radial_count // 2
        term = products[i * rows : (i + 1) * rows, :] * (
            filter_ref[first + i : first + i + 1, :] * math.exp(-0.5 * m * m)
        )
        total = term if total is None else total + term
    return total


def near_sum(tiles_ref, block_values, filter_ref, rows, group=4):
    radial_count = filter_ref.shape[0]
    total = None
    for first in range(0, radial_count, group):
        products = jnp.dot(
            tiles_ref[first * rows : (first + group) * rows, :],
            block_values,
            preferred_element_type=jnp.float32,
        )
        term = weighted(products, rows, first, filter_ref, radial_count)
        total = term if total is None else total + term
    return total


def near_kernel(
    where_ref, distances_ref, mask_ref, own_ref, sibling_ref, filter_ref, near_ref, far_tiles_ref, tiles_ref, *, step=32
):
    rows = distances_ref.shape[0]
    radial_count = filter_ref.shape[0]
    middle = radial_count // 2

    def make(block, target_ref, column):
        def one(i, carry):
            low = pl.multiple_of(i * step, step)
            start = pl.multiple_of(block * rows, rows)
            d = distances_ref[pl.ds(low, step), pl.ds(start, rows)]
            mask = mask_ref[pl.ds(low, step), pl.ds(start, rows)].astype(jnp.float32)
            u = d * (0.05 * 5.0 / radius_cut)
            half = horner(cos_terms, u * u)
            y = d * ((radial_count - 1) / radius_cut) - float(middle)
            centre = half * half * mask * jnp.exp(-0.5 * y * y)
            ratio = jnp.exp(y)
            back = jnp.exp(-y)

            def put(k, value):
                at = pl.multiple_of(k * rows + low, step)
                target_ref[pl.ds(at, step), column : column + rows] = value.astype(jnp.bfloat16)

            put(middle, centre)
            value = centre
            for k in range(middle + 1, radial_count):
                value = value * ratio
                put(k, value)
            value = centre
            for k in range(middle - 1, -1, -1):
                value = value * back
                put(k, value)
            return carry

        lax.fori_loop(0, rows // step, one, 0)

    make(1, tiles_ref, 0)
    make(where_ref[0], tiles_ref, rows)
    make(where_ref[1], far_tiles_ref, 0)
    block_values = jnp.concatenate([own_ref[:rows, :], sibling_ref[:rows, :]], axis=0)
    near_ref[...] = near_sum(tiles_ref, block_values, filter_ref, rows)


def last_kernel(
    pairs,
    nearby,
    choice_ref,
    wave_ref,
    sums_in_ref,
    filter_long_ref,
    own_phase_ref,
    near_in_ref,
    far_tiles_ref,
    filter_ref,
    *refs,
):
    chunks, near_chunks = refs[: 2 * pairs], refs[2 * pairs : 2 * pairs + nearby]
    near_ref, own_far_ref, message_ref, phase_ref, sums_ref, side_ref = refs[2 * pairs + nearby :]
    rows = near_ref.shape[0]
    for i in range(nearby):

        @pl.when(choice_ref[0] == i)
        def _():
            side_ref[...] = near_chunks[i][:rows, :]

    for i in range(pairs):
        base = sums_in_ref if i == 0 else sums_ref
        sums_ref[...] = base[...] + block_sums(
            phase_ref.at[i % 2], wave_ref, chunks[2 * i], chunks[2 * i + 1]
        )
    near_ref[...] = near_in_ref[...] + near_sum(far_tiles_ref, side_ref[...], filter_ref, rows)
    wave_count = wave_ref.shape[0]
    wave_weights = filter_long_ref[...]
    filtered = jnp.concatenate(
        [
            (sums_ref[:wave_count, :] * wave_weights).astype(jnp.bfloat16),
            (sums_ref[wave_count:, :] * wave_weights).astype(jnp.bfloat16),
        ],
        axis=0,
    )
    far = lax.dot_general(
        own_phase_ref[...],
        filtered,
        (((0,), (0,)), ((), ())),
        preferred_element_type=jnp.float32,
    )
    own_far_ref[...] = far[:rows, :]
    message_ref[...] = far[rows:, :].astype(jnp.bfloat16)


def update_kernel(
    scale,
    count_ref,
    features_ref,
    near_ref,
    own_far_ref,
    message_ref,
    gain_ref,
    w_inner_ref,
    w_outer_ref,
    out_ref,
):
    far = (own_far_ref[...] + message_ref[...].astype(jnp.float32)) * scale
    combined = features_ref[...].astype(jnp.float32) + near_ref[...] + far
    spread = lax.rsqrt(jnp.mean(combined * combined, axis=-1, keepdims=True) + 1e-06)
    normed = (combined * spread * gain_ref[...]).astype(jnp.bfloat16)
    inner = jnp.dot(normed, w_inner_ref[...], preferred_element_type=jnp.float32)
    inner = (inner / (1.0 + jnp.exp(-inner))).astype(jnp.bfloat16)
    result = jnp.dot(inner, w_outer_ref[...], preferred_element_type=jnp.float32)
    row = lax.broadcasted_iota(jnp.int32, result.shape, 0)
    out_ref[...] = jnp.where(row < count_ref[0], result, 0.0).astype(jnp.bfloat16)


vmem = pl.BlockSpec(memory_space=pltpu.VMEM)
smem = pl.BlockSpec(memory_space=pltpu.SMEM)


def call(kernel, name, specs, outs, scratch=(), flops=1_000_000, mib=8):
    shapes = tuple(jax.ShapeDtypeStruct(shape, dtype) for shape, dtype in outs)
    return pl.pallas_call(
        kernel,
        name=name,
        in_specs=specs,
        out_specs=tuple(vmem for _ in outs),
        out_shape=shapes,
        scratch_shapes=list(scratch),
        cost_estimate=pl.CostEstimate(flops=flops, bytes_accessed=1_000_000, transcendentals=0),
        compiler_params=pltpu.CompilerParams(vmem_limit_bytes=mib * 1024 * 1024),
    )


def gathered_body(
    features,
    positions,
    distances,
    pair_mask,
    counts,
    wave_index,
    w_value,
    filter_short,
    filter_long,
    gain,
    w_inner,
    w_outer,
):
    rows, width = features.shape
    radial_count = filter_short.shape[0]
    wave_count = wave_index.shape[1]
    blocks, cores = lax.axis_size("atoms"), lax.axis_size("waves")
    bf16, f32 = jnp.bfloat16, jnp.float32

    def across(mask):
        return [
            (a * cores + c, (a ^ mask) * cores + c) for a in range(blocks) for c in range(cores)
        ]

    over = [(a * cores + c, a * cores + 1 - c) for a in range(blocks) for c in range(cores)]
    block, core = lax.axis_index("atoms"), lax.axis_index("waves")

    chunk_rows = rows + extra_rows
    chunk, waves = call(
        prepare_kernel,
        "prepare",
        [smem, vmem, vmem, vmem, vmem],
        [((chunk_rows, width), bf16), ((wave_count, extra_rows), bf16)],
    )(counts, features, w_value, positions, wave_index)

    half = blocks // 2
    got = {0: chunk}
    if half:
        got[half] = lax.ppermute(chunk, both, across(half))
    for mask in range(half - 1, 0, -1):
        got[mask] = lax.ppermute(chunk, both, across(mask))
    for mask in range(half - 1, 0, -1):
        got[half ^ mask] = lax.ppermute(got[half], both, across(mask))
    other = {mask: lax.ppermute(value, both, over) for mask, value in got.items()}

    sums_shape = ((2 * wave_count, width), f32)
    phase_shape = (2 * wave_count, 2 * rows)
    sums, own_phase = call(
        own_kernel, "own_sums", [vmem] * 3, [sums_shape, (phase_shape, bf16)]
    )(waves, chunk, other[0])
    (wave_weights,) = call(
        functools.partial(filter_kernel, float(rows * blocks * cores) ** -0.5),
        "wave_filter",
        [vmem, vmem],
        [((wave_count, width), f32)],
    )(wave_index, filter_long)

    sibling_block = 2 - 2 * core
    where = jnp.stack([sibling_block, 2 - sibling_block]).astype(jnp.int32)
    near, far_tiles = call(
        near_kernel,
        "near",
        [smem] + [vmem] * 5,
        [((rows, width), f32), ((radial_count * rows, rows), bf16)],
        [pltpu.VMEM((radial_count * rows, 2 * rows), bf16)],
        mib=16,
    )(where, distances, pair_mask, chunk, other[0], filter_short)

    def more(sums, masks):
        chunks = [c for mask in masks for c in (got[mask], other[mask])]
        return call(
            functools.partial(more_kernel, len(masks)),
            "more_sums",
            [vmem] * (2 + len(chunks)),
            [sums_shape],
            [pltpu.VMEM((2,) + phase_shape, bf16)],
        )(waves, sums, *chunks)[0]

    if half > 1:
        sums = more(sums, list(range(1, half)))
    last = [half ^ mask for mask in range(half - 1, 0, -1)]
    if half:
        sums = more(sums, [half])

    masks = sorted({a ^ ((a + 1) % blocks) for a in range(blocks)})
    mask = block ^ ((block + 2 * core - 1 + blocks) % blocks)
    choice = sum(jnp.where(mask == m, i, 0) for i, m in enumerate(masks))
    choice = jnp.reshape(choice, (1,)).astype(jnp.int32)
    chunks = [c for m in last for c in (got[m], other[m])]
    near_chunks = [other[m] for m in masks]
    near, own_far, message = call(
        functools.partial(last_kernel, len(last), len(masks)),
        "last_sums",
        [smem] + [vmem] * (7 + len(chunks) + len(near_chunks)),
        [((rows, width), f32), ((rows, width), f32), ((rows, width), bf16)],
        [
            pltpu.VMEM((2,) + phase_shape, bf16),
            pltpu.VMEM(sums_shape[0], f32),
            pltpu.VMEM((rows, width), bf16),
        ],
        mib=12,
    )(
        choice,
        waves,
        sums,
        wave_weights,
        own_phase,
        near,
        far_tiles,
        filter_short,
        *chunks,
        *near_chunks,
    )
    message = lax.ppermute(message, both, over)
    return call(
        functools.partial(update_kernel, float(wave_count * cores) ** -0.5),
        "update",
        [smem] + [vmem] * 7,
        [((rows, width), bf16)],
    )(counts, features, near, own_far, message, jnp.reshape(gain, (1, width)), w_inner, w_outer)[0]


def gathers(mesh):
    blocks, cores = mesh.shape["atoms"], mesh.shape["waves"]
    return cores == 2 and blocks <= gather_limit and blocks & (blocks - 1) == 0


def solution(mesh):
    placed = (
        P(("groups", "atoms", "waves"), None),
        P(None, ("groups", "atoms", "waves")),
        P(("groups", "atoms", "waves"), None),
        P(("groups", "atoms", "waves"), None),
        P(("groups", "atoms", "waves")),
        P(None, ("groups", "waves")),
        P(),
        P(),
        P(),
        P(),
        P(),
        P(),
    )
    return jax.shard_map(
        gathered_body if gathers(mesh) else summed_body,
        mesh=mesh,
        in_specs=placed,
        out_specs=P(("groups", "atoms", "waves"), None),
        check_vma=False,
    )
```

```python
import functools
import math

import jax
import jax.numpy as jnp
from jax import lax
from jax.experimental import pallas as pl
from jax.experimental.pallas import tpu as pltpu
from jax.sharding import PartitionSpec as P

radius_cut = 5.0
wave_top = 6.0 * 3.0**0.5
both = ("atoms", "waves")
gather_limit = 8
extra_rows = 16

sin_terms = (
    2.641753992459813,
    -1.08637674632807,
    0.134005627536115,
    -0.007739884914760742,
)


def padded(block, sides, width):
    for axis, dim in sides:
        count = lax.axis_size(axis)
        forward = [(i, i + 1) for i in range(count - 1)]
        forward.append((count - 1, 0))
        backward = [(target, source) for source, target in forward]
        low = lax.ppermute(
            lax.slice_in_dim(block, block.shape[dim] - width, None, axis=dim), axis, forward
        )
        high = lax.ppermute(lax.slice_in_dim(block, 0, width, axis=dim), axis, backward)
        block = jnp.concatenate([low, block, high], axis=dim)
    return block


def radial_tiles(distances, pair_mask, radial_count):
    centres = radius_cut * jnp.arange(radial_count, dtype=jnp.float32) / (radial_count - 1)
    spacing = radius_cut / (radial_count - 1)
    envelope = (
        0.5 * (jnp.cos(jnp.pi * distances / radius_cut) + 1.0) * pair_mask.astype(jnp.float32)
    )
    offsets = (distances[None] - centres[:, None, None]) / spacing
    tiles = jnp.exp(-0.5 * offsets * offsets) * envelope[None]
    return tiles.astype(jnp.bfloat16)


def phase_tiles(points, wave_index):
    waves = wave_index.astype(jnp.float32)
    theta = points[0][:, None] * waves[0][None, :] + points[1][:, None] * waves[1][None, :]
    theta = 2.0 * jnp.pi * (theta + points[2][:, None] * waves[2][None, :])
    return (jnp.cos(theta).astype(jnp.bfloat16), jnp.sin(theta).astype(jnp.bfloat16))


def wave_filter(wave_index, filter_long):
    waves = wave_index.astype(jnp.float32)
    radial_count = filter_long.shape[0]
    magnitude = jnp.sqrt(waves[0] * waves[0] + waves[1] * waves[1] + waves[2] * waves[2])
    centres = wave_top * jnp.arange(radial_count, dtype=jnp.float32) / (radial_count - 1)
    spacing = wave_top / (radial_count - 1)
    offsets = (magnitude[None, :] - centres[:, None]) / spacing
    k_basis = jnp.exp(-0.5 * offsets * offsets)
    return jnp.dot(k_basis.T, filter_long, precision=lax.Precision.HIGHEST)


def summed_body(
    features,
    positions,
    distances,
    pair_mask,
    counts,
    wave_index,
    w_value,
    filter_short,
    filter_long,
    gain,
    w_inner,
    w_outer,
):
    row_count = features.shape[0]
    width = features.shape[1]
    radial_count = filter_short.shape[0]
    occupied = (lax.iota(jnp.int32, row_count) < counts[0]).astype(jnp.float32)
    values = (
        jnp.dot(features, w_value, preferred_element_type=jnp.float32) * occupied[:, None]
    ).astype(jnp.bfloat16)
    beside_all = padded(values, ((("atoms", "waves"), 0),), row_count)
    tiles = radial_tiles(distances, pair_mask, radial_count).reshape(
        radial_count * row_count, 3 * row_count
    )
    products = jnp.dot(tiles, beside_all, preferred_element_type=jnp.float32).reshape(
        radial_count, row_count, width
    )
    near_field = jnp.sum(products * filter_short[:, None, :], axis=0)
    wide_values, block_points = (
        lax.all_gather(values.astype(jnp.float32), "waves", axis=0, tiled=True),
        lax.all_gather(positions, "waves", axis=1, tiled=True),
    )
    block_values = wide_values.astype(jnp.bfloat16)
    cosine, sine = phase_tiles(block_points, wave_index)
    cos_sum = jnp.einsum("ak,af->kf", cosine, block_values, preferred_element_type=jnp.float32)
    sin_sum = jnp.einsum("ak,af->kf", sine, block_values, preferred_element_type=jnp.float32)
    atom_total = row_count * lax.axis_size(("atoms", "waves"))
    wave_total = wave_index.shape[1] * lax.axis_size("waves")
    factor_scale = float(atom_total) ** (-0.5)
    cos_total, sin_total = lax.psum((cos_sum, sin_sum), "atoms")
    block_filter = wave_filter(wave_index, filter_long)
    cos_filtered = (cos_total * block_filter * factor_scale).astype(jnp.bfloat16)
    sin_filtered = (sin_total * block_filter * factor_scale).astype(jnp.bfloat16)
    far_field = lax.psum_scatter(
        (
            jnp.dot(cosine, cos_filtered, preferred_element_type=jnp.float32)
            + jnp.dot(sine, sin_filtered, preferred_element_type=jnp.float32)
        ).astype(jnp.bfloat16),
        "waves",
        scatter_dimension=0,
        tiled=True,
    ).astype(jnp.float32) * float(wave_total) ** (-0.5)
    combined = features.astype(jnp.float32) + near_field + far_field
    normed = (
        combined * lax.rsqrt(jnp.mean(combined * combined, axis=-1, keepdims=True) + 1e-06) * gain
    ).astype(jnp.bfloat16)
    inner = jax.nn.silu(jnp.dot(normed, w_inner, preferred_element_type=jnp.float32)).astype(
        jnp.bfloat16
    )
    result = jnp.dot(inner, w_outer, preferred_element_type=jnp.float32) * occupied[:, None]
    return result.astype(jnp.bfloat16)


def horner(terms, w):
    total = jnp.full_like(w, terms[-1])
    for term in terms[-2::-1]:
        total = total * w + term
    return total


def phases(turns):
    r = turns - jnp.round(turns)
    quarter = r * horner(sin_terms, r * r)
    square = quarter * quarter
    rest = 2.0**1.5 - square
    half_sin = quarter * (rest * lax.rsqrt(rest))
    half_cos = 2.0**0.5 - square
    return 1.0 - half_sin * half_sin, half_sin * half_cos


def fill_phases(phase_ref, column, wave_ref, point_rows, step=64):
    wave_count = wave_ref.shape[0]
    width = point_rows.shape[1]
    for low in range(0, wave_count, step):
        turns = jnp.dot(
            wave_ref[low : low + step, :], point_rows, preferred_element_type=jnp.float32
        )
        cosine, sine = phases(turns)
        phase_ref[low : low + step, column : column + width] = cosine.astype(jnp.bfloat16)
        phase_ref[wave_count + low : wave_count + low + step, column : column + width] = (
            sine.astype(jnp.bfloat16)
        )


def add_sums(sums, chunks, wave_ref, phase_ref):
    rows = chunks[0].shape[0] - extra_rows
    for i in range(len(chunks) // 2):
        first, second = chunks[2 * i], chunks[2 * i + 1]
        slot = phase_ref.at[i % 2]
        fill_phases(slot, 0, wave_ref, first[rows:, :])
        fill_phases(slot, rows, wave_ref, second[rows:, :])
        block_values = jnp.concatenate([first[:rows, :], second[:rows, :]], axis=0)
        found = jnp.dot(slot[...], block_values, preferred_element_type=jnp.float32)
        sums = found if sums is None else sums + found
    return sums


def fetch(sources, targets, semaphores):
    copies = [
        pltpu.make_async_copy(source, target, semaphores.at[i])
        for i, (source, target) in enumerate(zip(sources, targets))
    ]
    for copy in copies:
        copy.start()
    for copy in copies:
        copy.wait()


def prepare_kernel(
    features_hbm,
    w_value_hbm,
    positions_hbm,
    count_hbm,
    chunk_ref,
    features,
    w_value,
    positions,
    count_ref,
    sems,
):
    fetch(
        (features_hbm, w_value_hbm, positions_hbm, count_hbm),
        (features, w_value, positions, count_ref),
        sems,
    )
    rows = features.shape[0]
    values = jnp.dot(features[...], w_value[...], preferred_element_type=jnp.float32)
    row = lax.broadcasted_iota(jnp.int32, values.shape, 0)
    chunk_ref[:rows, :] = jnp.where(row < count_ref[0], values, 0.0).astype(jnp.bfloat16)
    points = positions[...]
    high = points.astype(jnp.bfloat16).astype(jnp.float32)
    middle = (points - high).astype(jnp.bfloat16).astype(jnp.float32)
    low = points - high - middle
    spare = jnp.zeros((extra_rows - 9, rows), jnp.float32)
    chunk_ref[rows:, :] = jnp.concatenate([high, middle, low, spare], axis=0).astype(jnp.bfloat16)


def waves_kernel(
    scale, wave_hbm, filter_long_hbm, waves_ref, weights_ref, wave_ref, filter_long_ref, sems
):
    fetch((wave_hbm, filter_long_hbm), (wave_ref, filter_long_ref), sems)
    waves = wave_ref[...].astype(jnp.float32)
    spare = jnp.zeros((extra_rows - 9, waves.shape[1]), jnp.float32)
    waves_ref[...] = jnp.concatenate([waves, waves, waves, spare], axis=0).T.astype(jnp.bfloat16)
    radial_count = filter_long_ref.shape[0]
    magnitude = jnp.sqrt(
        waves[0:1] * waves[0:1] + waves[1:2] * waves[1:2] + waves[2:3] * waves[2:3]
    )
    spacing = wave_top / (radial_count - 1)
    index = lax.broadcasted_iota(jnp.int32, (radial_count, waves.shape[1]), 0)
    offsets = magnitude / spacing - index.astype(jnp.float32)
    basis = jnp.exp(-0.5 * offsets * offsets)
    weights_ref[...] = scale * jnp.dot(
        basis.T,
        filter_long_ref[...],
        precision=lax.Precision.HIGHEST,
        preferred_element_type=jnp.float32,
    )


def own_kernel(wave_ref, first_ref, second_ref, sums_ref, turned_ref, phase_ref):
    sums_ref[...] = add_sums(None, (first_ref, second_ref), wave_ref, phase_ref)
    turned_ref[...] = phase_ref[0].T


def more_kernel(wave_ref, sums_in_ref, *refs):
    chunks, (sums_ref, phase_ref) = refs[:-2], refs[-2:]
    sums_ref[...] = add_sums(sums_in_ref[...], chunks, wave_ref, phase_ref)


def weighted(products, rows, filter_ref):
    radial_count = filter_ref.shape[0]
    total = None
    for k in range(radial_count):
        m = k - radial_count // 2
        term = products[k * rows : (k + 1) * rows, :] * (
            filter_ref[k : k + 1, :] * math.exp(-0.5 * m * m)
        )
        total = term if total is None else total + term
    return total


def near_kernel(
    distances_ref,
    mask_ref,
    filter_ref,
    own_ref,
    sibling_ref,
    near_ref,
    far_tiles_ref,
    tiles_ref,
    *,
    step,
    part=32,
):
    rows = distances_ref.shape[0]
    radial_count = filter_ref.shape[0]
    middle = radial_count // 2
    sibling = 2 - 2 * lax.axis_index("waves")

    def make(low, block, put):
        start = block * rows if isinstance(block, int) else pl.multiple_of(block * rows, rows)
        d = distances_ref[low : low + part, pl.ds(start, rows)]
        mask = mask_ref[low : low + part, pl.ds(start, rows)].astype(jnp.float32)
        u = d * (0.5 / radius_cut)
        quarter = u * horner(sin_terms, u * u)
        half = 1.0 - 0.5**0.5 * quarter * quarter
        y = d * ((radial_count - 1) / radius_cut) - float(middle)
        centre = half * half * mask * jnp.exp(-0.5 * y * y)
        ratio = jnp.exp(y)
        back = jnp.exp(-y)
        put(middle, centre.astype(jnp.bfloat16))
        value = centre
        for k in range(middle + 1, radial_count):
            value = value * ratio
            put(k, value.astype(jnp.bfloat16))
        value = centre
        for k in range(middle - 1, -1, -1):
            value = value * back
            put(k, value.astype(jnp.bfloat16))

    block_values = jnp.concatenate([own_ref[:rows, :], sibling_ref[:rows, :]], axis=0)

    def products(i):
        found = jnp.dot(tiles_ref[i % 2], block_values, preferred_element_type=jnp.float32)
        near_ref[i * step : (i + 1) * step, :] = weighted(found, step, filter_ref)

    for i in range(rows // step):
        for low in range(i * step, (i + 1) * step, part):
            inner = low - i * step

            def put(column):
                def store(k, value):
                    at = k * step + inner
                    tiles_ref[i % 2, at : at + part, column : column + rows] = value

                return store

            def put_far(k, value):
                at = k * rows + low
                far_tiles_ref[at : at + part, :] = value

            make(low, 1, put(0))
            make(low, sibling, put(rows))
            make(low, 2 - sibling, put_far)
        if i:
            products(i - 1)
    products(rows // step - 1)


def beyond_kernel(nearby, near_in_ref, far_tiles_ref, filter_ref, *refs):
    near_chunks, (near_ref, side_ref) = refs[:nearby], refs[nearby:]
    rows = near_ref.shape[0]
    blocks, block = lax.axis_size("atoms"), lax.axis_index("atoms")
    side = lax.rem(block + 2 * lax.axis_index("waves") - 1 + blocks, blocks)
    for mask, chunk in zip(near_masks(blocks), near_chunks):

        @pl.when((block ^ side) == mask)
        def _():
            side_ref[...] = chunk[:rows, :]

    found = jnp.dot(far_tiles_ref[...], side_ref[...], preferred_element_type=jnp.float32)
    near_ref[...] = near_in_ref[...] + weighted(found, rows, filter_ref)


def near_masks(blocks):
    return sorted({a ^ ((a + 1) % blocks) for a in range(blocks)})


def last_kernel(
    wave_ref,
    sums_in_ref,
    weights_ref,
    turned_ref,
    *refs,
):
    chunks, (own_far_ref, message_ref, phase_ref) = refs[:-3], refs[-3:]
    rows = own_far_ref.shape[0]
    wave_count = wave_ref.shape[0]
    sums = add_sums(sums_in_ref[...], chunks, wave_ref, phase_ref)
    weights = weights_ref[...]
    filtered = jnp.concatenate(
        [
            (sums[:wave_count, :] * weights).astype(jnp.bfloat16),
            (sums[wave_count:, :] * weights).astype(jnp.bfloat16),
        ],
        axis=0,
    )
    far = jnp.dot(turned_ref[...], filtered, preferred_element_type=jnp.float32)
    own_far_ref[...] = far[:rows, :]
    message_ref[...] = far[rows:, :].astype(jnp.bfloat16)


def update_kernel(
    scale,
    count_hbm,
    features_ref,
    near_ref,
    own_far_ref,
    message_ref,
    gain_ref,
    w_inner_ref,
    w_outer_ref,
    out_ref,
    count_ref,
    sem,
):
    copy = pltpu.make_async_copy(count_hbm, count_ref, sem)
    copy.start()
    far = (own_far_ref[...] + message_ref[...].astype(jnp.float32)) * scale
    combined = features_ref[...].astype(jnp.float32) + near_ref[...] + far
    spread = lax.rsqrt(jnp.mean(combined * combined, axis=-1, keepdims=True) + 1e-06)
    normed = (combined * spread * gain_ref[...]).astype(jnp.bfloat16)
    inner = jnp.dot(normed, w_inner_ref[...], preferred_element_type=jnp.float32)
    inner = (inner / (1.0 + jnp.exp(-inner))).astype(jnp.bfloat16)
    result = jnp.dot(inner, w_outer_ref[...], preferred_element_type=jnp.float32)
    row = lax.broadcasted_iota(jnp.int32, result.shape, 0)
    copy.wait()
    out_ref[...] = jnp.where(row < count_ref[0], result, 0.0).astype(jnp.bfloat16)


hbm = pl.BlockSpec(memory_space=pltpu.HBM)
vmem = pl.BlockSpec(memory_space=pltpu.VMEM)


def call(kernel, specs, outs, scratch=(), micros=1.0, mib=8):
    shapes = tuple(jax.ShapeDtypeStruct(shape, dtype) for shape, dtype in outs)
    return pl.pallas_call(
        kernel,
        in_specs=specs,
        out_specs=tuple(vmem for _ in outs),
        out_shape=shapes,
        scratch_shapes=list(scratch),
        cost_estimate=pl.CostEstimate(
            flops=int(micros * 1.1e9), bytes_accessed=int(micros * 1e6), transcendentals=0
        ),
        compiler_params=pltpu.CompilerParams(vmem_limit_bytes=mib * 1024 * 1024),
    )


def gathered_parts(
    features,
    positions,
    distances,
    pair_mask,
    counts,
    wave_index,
    w_value,
    filter_short,
    filter_long,
    gain,
    w_inner,
    w_outer,
):
    rows, width = features.shape
    radial_count = filter_short.shape[0]
    wave_count = wave_index.shape[1]
    blocks, cores = lax.axis_size("atoms"), lax.axis_size("waves")
    bf16, f32 = jnp.bfloat16, jnp.float32

    def across(mask):
        return [
            (a * cores + c, (a ^ mask) * cores + c) for a in range(blocks) for c in range(cores)
        ]

    over = [(a * cores + c, a * cores + 1 - c) for a in range(blocks) for c in range(cores)]

    chunk_rows = rows + extra_rows
    (chunk,) = call(
        prepare_kernel,
        [hbm, hbm, hbm, hbm],
        [((chunk_rows, width), bf16)],
        [
            pltpu.VMEM(features.shape, features.dtype),
            pltpu.VMEM(w_value.shape, w_value.dtype),
            pltpu.VMEM(positions.shape, positions.dtype),
            pltpu.SMEM(counts.shape, counts.dtype),
            pltpu.SemaphoreType.DMA((4,)),
        ],
        micros=1.0,
        mib=60,
    )(features, w_value, positions, counts)
    waves, wave_weights = call(
        functools.partial(waves_kernel, float(rows * blocks * cores) ** -0.5),
        [hbm, hbm],
        [((wave_count, extra_rows), bf16), ((wave_count, width), f32)],
        [
            pltpu.VMEM(wave_index.shape, wave_index.dtype),
            pltpu.VMEM(filter_long.shape, filter_long.dtype),
            pltpu.SemaphoreType.DMA((2,)),
        ],
        micros=1.3,
    )(wave_index, filter_long)

    half = blocks // 2

    def move(value, mask):
        return lax.ppermute(value, both, across(mask))

    got = {0: chunk, half: move(chunk, half)}
    for mask in range(half - 1, 0, -1):
        got[mask] = move(chunk, mask)
    for mask in range(half - 1, 0, -1):
        got[half ^ mask] = move(got[half], mask)
    other = {}
    for mask, value in got.items():
        other[mask] = lax.ppermute(value, both, over)

    sums_shape = ((2 * wave_count, width), f32)
    phase_shape = (2 * wave_count, 2 * rows)
    sums, turned = call(
        own_kernel,
        [vmem] * 3,
        [sums_shape, (phase_shape[::-1], bf16)],
        [pltpu.VMEM((1,) + phase_shape, bf16)],
        micros=1.0,
    )(waves, chunk, other[0])

    step = rows // 4
    near, far_tiles = call(
        functools.partial(near_kernel, step=step),
        [vmem] * 5,
        [((rows, width), f32), ((radial_count * rows, rows), bf16)],
        [pltpu.VMEM((2, radial_count * step, 2 * rows), bf16)],
        micros=2.5,
        mib=16,
    )(distances, pair_mask, filter_short, chunk, other[0])

    def pairs(masks):
        return [c for mask in masks for c in (got[mask], other[mask])]

    groups = sum_groups(blocks)
    for masks in groups[:-1]:
        (sums,) = call(
            more_kernel,
            [vmem] * (2 + 2 * len(masks)),
            [sums_shape],
            [pltpu.VMEM((min(2, len(masks)),) + phase_shape, bf16)],
            micros=0.8 * len(masks) + 0.3,
            mib=12,
        )(waves, sums, *pairs(masks))
    own_far, message = call(
        last_kernel,
        [vmem] * (4 + 2 * len(groups[-1])),
        [((rows, width), f32), ((rows, width), bf16)],
        [pltpu.VMEM((min(2, len(groups[-1])),) + phase_shape, bf16)],
        micros=1.5,
        mib=12,
    )(waves, sums, wave_weights, turned, *pairs(groups[-1]))
    message = lax.ppermute(message, both, over)
    near_chunks = [other[m] for m in near_masks(blocks)]
    (near,) = call(
        functools.partial(beyond_kernel, len(near_chunks)),
        [vmem] * (3 + len(near_chunks)),
        [((rows, width), f32)],
        [pltpu.VMEM((rows, width), bf16)],
        micros=1.0,
        mib=12,
    )(near, far_tiles, filter_short, *near_chunks)
    return call(
        functools.partial(update_kernel, float(wave_count * cores) ** -0.5),
        [hbm] + [vmem] * 7,
        [((rows, width), bf16)],
        [pltpu.SMEM(counts.shape, counts.dtype), pltpu.SemaphoreType.DMA],
        micros=1.0,
    )(counts, features, near, own_far, message, jnp.reshape(gain, (1, width)), w_inner, w_outer)[0]


def gathered_body(*args):
    return gathered_parts(*args)


def move_masks(blocks):
    half = blocks // 2
    direct = list(range(half - 1, 0, -1))
    return [half] + direct, [half ^ mask for mask in direct]


def sum_groups(blocks):
    starts, passed = move_masks(blocks)
    order = starts[:1] + passed
    groups = [starts[1:], order[:2]] + [[mask] for mask in order[2:]]
    return [group for group in groups if group]


def gathers(mesh):
    blocks, cores = mesh.shape["atoms"], mesh.shape["waves"]
    return cores == 2 and 2 <= blocks <= gather_limit and blocks & (blocks - 1) == 0


def solution(mesh):
    placed = (
        P(("groups", "atoms", "waves"), None),
        P(None, ("groups", "atoms", "waves")),
        P(("groups", "atoms", "waves"), None),
        P(("groups", "atoms", "waves"), None),
        P(("groups", "atoms", "waves")),
        P(None, ("groups", "waves")),
        P(),
        P(),
        P(),
        P(),
        P(),
        P(),
    )
    return jax.shard_map(
        gathered_body if gathers(mesh) else summed_body,
        mesh=mesh,
        in_specs=placed,
        out_specs=P(("groups", "atoms", "waves"), None),
        check_vma=False,
    )
```

```python
import functools
import math

import jax
import jax.numpy as jnp
from jax import lax
from jax.experimental import pallas as pl
from jax.experimental.pallas import tpu as pltpu
from jax.sharding import PartitionSpec as P

radius_cut = 5.0
wave_top = 6.0 * 3.0**0.5
both = ("atoms", "waves")
gather_limit = 8
extra_rows = 16

sin_terms = (2.641737538071335, -1.0859062893731768, 0.13047468843565363)


def padded(block, sides, width):
    for axis, dim in sides:
        count = lax.axis_size(axis)
        forward = [(i, i + 1) for i in range(count - 1)]
        forward.append((count - 1, 0))
        backward = [(target, source) for source, target in forward]
        low = lax.ppermute(
            lax.slice_in_dim(block, block.shape[dim] - width, None, axis=dim), axis, forward
        )
        high = lax.ppermute(lax.slice_in_dim(block, 0, width, axis=dim), axis, backward)
        block = jnp.concatenate([low, block, high], axis=dim)
    return block


def radial_tiles(distances, pair_mask, radial_count):
    centres = radius_cut * jnp.arange(radial_count, dtype=jnp.float32) / (radial_count - 1)
    spacing = radius_cut / (radial_count - 1)
    envelope = (
        0.5 * (jnp.cos(jnp.pi * distances / radius_cut) + 1.0) * pair_mask.astype(jnp.float32)
    )
    offsets = (distances[None] - centres[:, None, None]) / spacing
    tiles = jnp.exp(-0.5 * offsets * offsets) * envelope[None]
    return tiles.astype(jnp.bfloat16)


def phase_tiles(points, wave_index):
    waves = wave_index.astype(jnp.float32)
    theta = points[0][:, None] * waves[0][None, :] + points[1][:, None] * waves[1][None, :]
    theta = 2.0 * jnp.pi * (theta + points[2][:, None] * waves[2][None, :])
    return (jnp.cos(theta).astype(jnp.bfloat16), jnp.sin(theta).astype(jnp.bfloat16))


def wave_filter(wave_index, filter_long):
    waves = wave_index.astype(jnp.float32)
    radial_count = filter_long.shape[0]
    magnitude = jnp.sqrt(waves[0] * waves[0] + waves[1] * waves[1] + waves[2] * waves[2])
    centres = wave_top * jnp.arange(radial_count, dtype=jnp.float32) / (radial_count - 1)
    spacing = wave_top / (radial_count - 1)
    offsets = (magnitude[None, :] - centres[:, None]) / spacing
    k_basis = jnp.exp(-0.5 * offsets * offsets)
    return jnp.dot(k_basis.T, filter_long, precision=lax.Precision.HIGHEST)


def summed_body(
    features,
    positions,
    distances,
    pair_mask,
    counts,
    wave_index,
    w_value,
    filter_short,
    filter_long,
    gain,
    w_inner,
    w_outer,
):
    row_count = features.shape[0]
    width = features.shape[1]
    radial_count = filter_short.shape[0]
    occupied = (lax.iota(jnp.int32, row_count) < counts[0]).astype(jnp.float32)
    values = (
        jnp.dot(features, w_value, preferred_element_type=jnp.float32) * occupied[:, None]
    ).astype(jnp.bfloat16)
    beside_all = padded(values, ((("atoms", "waves"), 0),), row_count)
    tiles = radial_tiles(distances, pair_mask, radial_count).reshape(
        radial_count * row_count, 3 * row_count
    )
    products = jnp.dot(tiles, beside_all, preferred_element_type=jnp.float32).reshape(
        radial_count, row_count, width
    )
    near_field = jnp.sum(products * filter_short[:, None, :], axis=0)
    wide_values, block_points = (
        lax.all_gather(values.astype(jnp.float32), "waves", axis=0, tiled=True),
        lax.all_gather(positions, "waves", axis=1, tiled=True),
    )
    block_values = wide_values.astype(jnp.bfloat16)
    cosine, sine = phase_tiles(block_points, wave_index)
    cos_sum = jnp.einsum("ak,af->kf", cosine, block_values, preferred_element_type=jnp.float32)
    sin_sum = jnp.einsum("ak,af->kf", sine, block_values, preferred_element_type=jnp.float32)
    atom_total = row_count * lax.axis_size(("atoms", "waves"))
    wave_total = wave_index.shape[1] * lax.axis_size("waves")
    factor_scale = float(atom_total) ** (-0.5)
    cos_total, sin_total = lax.psum((cos_sum, sin_sum), "atoms")
    block_filter = wave_filter(wave_index, filter_long)
    cos_filtered = (cos_total * block_filter * factor_scale).astype(jnp.bfloat16)
    sin_filtered = (sin_total * block_filter * factor_scale).astype(jnp.bfloat16)
    far_field = lax.psum_scatter(
        (
            jnp.dot(cosine, cos_filtered, preferred_element_type=jnp.float32)
            + jnp.dot(sine, sin_filtered, preferred_element_type=jnp.float32)
        ).astype(jnp.bfloat16),
        "waves",
        scatter_dimension=0,
        tiled=True,
    ).astype(jnp.float32) * float(wave_total) ** (-0.5)
    combined = features.astype(jnp.float32) + near_field + far_field
    normed = (
        combined * lax.rsqrt(jnp.mean(combined * combined, axis=-1, keepdims=True) + 1e-06) * gain
    ).astype(jnp.bfloat16)
    inner = jax.nn.silu(jnp.dot(normed, w_inner, preferred_element_type=jnp.float32)).astype(
        jnp.bfloat16
    )
    result = jnp.dot(inner, w_outer, preferred_element_type=jnp.float32) * occupied[:, None]
    return result.astype(jnp.bfloat16)


def horner(terms, w):
    total = jnp.full_like(w, terms[-1])
    for term in terms[-2::-1]:
        total = total * w + term
    return total


def phases(turns):
    r = turns - jnp.round(turns)
    quarter = r * horner(sin_terms, r * r)
    square = quarter * quarter
    rest = 2.0**1.5 - square
    half_sin = quarter * (rest * lax.rsqrt(rest))
    half_cos = 2.0**0.5 - square
    return 1.0 - half_sin * half_sin, half_sin * half_cos


def add_sums(sums_in, sums_ref, chunks, wave_ref, phase_ref, turned_ref=None, block=128, step=64):
    rows = chunks[0].shape[0] - extra_rows
    wave_count = wave_ref.shape[0]
    block_values = [chunk[:rows, :] for chunk in chunks]
    block_values = jnp.concatenate(block_values, axis=0) if len(chunks) > 1 else block_values[0]
    for index, start in enumerate(range(0, wave_count, block)):
        slot = phase_ref.at[index % 2]
        for i, chunk in enumerate(chunks):
            part = slice(i * rows, (i + 1) * rows)
            for low in range(0, block, step):
                turns = jnp.dot(
                    wave_ref[start + low : start + low + step, :],
                    chunk[rows:, :],
                    preferred_element_type=jnp.float32,
                )
                cosine, sine = phases(turns)
                slot[low : low + step, part] = cosine.astype(jnp.bfloat16)
                slot[block + low : block + low + step, part] = sine.astype(jnp.bfloat16)
        found = jnp.dot(slot[...], block_values, preferred_element_type=jnp.float32)
        for first, rank in ((start, 0), (wave_count + start, block)):
            value = found[rank : rank + block, :]
            if sums_in is not None:
                value = sums_in[first : first + block, :] + value
            sums_ref[first : first + block, :] = value
            if turned_ref is not None:
                turned_ref[:, first : first + block] = slot[rank : rank + block, :rows].T


def fetch(sources, targets, semaphores):
    copies = [
        pltpu.make_async_copy(source, target, semaphores.at[i])
        for i, (source, target) in enumerate(zip(sources, targets))
    ]
    for copy in copies:
        copy.start()
    for copy in copies:
        copy.wait()


def prepare_kernel(
    features_hbm,
    w_value_hbm,
    positions_hbm,
    count_hbm,
    chunk_ref,
    features,
    w_value,
    positions,
    count_ref,
    sems,
):
    fetch(
        (features_hbm, w_value_hbm, positions_hbm, count_hbm),
        (features, w_value, positions, count_ref),
        sems,
    )
    rows = features.shape[0]
    values = jnp.dot(features[...], w_value[...], preferred_element_type=jnp.float32)
    row = lax.broadcasted_iota(jnp.int32, values.shape, 0)
    chunk_ref[:rows, :] = jnp.where(row < count_ref[0], values, 0.0).astype(jnp.bfloat16)
    points = positions[...]
    high = points.astype(jnp.bfloat16).astype(jnp.float32)
    middle = (points - high).astype(jnp.bfloat16).astype(jnp.float32)
    low = points - high - middle
    spare = jnp.zeros((extra_rows - 9, rows), jnp.float32)
    chunk_ref[rows:, :] = jnp.concatenate([high, middle, low, spare], axis=0).astype(jnp.bfloat16)


def waves_kernel(
    scale, own_wave_ref, other_wave_ref, filter_long_ref, waves_ref, weights_ref
):
    waves = jnp.concatenate([own_wave_ref[...], other_wave_ref[...]], axis=1).astype(jnp.float32)
    spare = jnp.zeros((extra_rows - 9, waves.shape[1]), jnp.float32)
    waves_ref[...] = jnp.concatenate([waves, waves, waves, spare], axis=0).T.astype(jnp.bfloat16)
    radial_count = filter_long_ref.shape[0]
    magnitude = jnp.sqrt(
        waves[0:1] * waves[0:1] + waves[1:2] * waves[1:2] + waves[2:3] * waves[2:3]
    )
    spacing = wave_top / (radial_count - 1)
    index = lax.broadcasted_iota(jnp.int32, (radial_count, waves.shape[1]), 0)
    offsets = magnitude / spacing - index.astype(jnp.float32)
    basis = jnp.exp(-0.5 * offsets * offsets)
    weights_ref[...] = scale * jnp.dot(
        basis.T,
        filter_long_ref[...],
        precision=lax.Precision.HIGHEST,
        preferred_element_type=jnp.float32,
    )


def first_kernel(wave_ref, *refs):
    chunks, (sums_ref, turned_ref, phase_ref) = refs[:-3], refs[-3:]
    add_sums(None, sums_ref, chunks, wave_ref, phase_ref, turned_ref)


def last_kernel(wave_ref, sums_in_ref, weights_ref, *refs):
    chunks, (shared_ref, phase_ref, sums_ref) = refs[:-3], refs[-3:]
    add_sums(sums_in_ref, sums_ref, chunks, wave_ref, phase_ref)
    wave_count = wave_ref.shape[0]
    for start in (0, wave_count):
        part = slice(start, start + wave_count)
        shared_ref[part, :] = (sums_ref[part, :] * weights_ref[...]).astype(jnp.bfloat16)


def weighted(products, rows, filter_ref):
    radial_count = filter_ref.shape[0]
    total = None
    for k in range(radial_count):
        m = k - radial_count // 2
        term = products[k * rows : (k + 1) * rows, :] * (
            filter_ref[k : k + 1, :] * math.exp(-0.5 * m * m)
        )
        total = term if total is None else total + term
    return total


def near_kernel(
    distances_ref,
    mask_ref,
    filter_ref,
    own_ref,
    near_ref,
    far_tiles_ref,
    tiles_ref,
    *,
    step,
    part=32,
):
    rows = distances_ref.shape[0]
    radial_count = filter_ref.shape[0]
    middle = radial_count // 2
    sibling = 2 - 2 * lax.axis_index("waves")

    def make(low, block, put):
        start = block * rows if isinstance(block, int) else pl.multiple_of(block * rows, rows)
        d = distances_ref[low : low + part, pl.ds(start, rows)]
        mask = mask_ref[low : low + part, pl.ds(start, rows)].astype(jnp.float32)
        u = d * (0.5 / radius_cut)
        quarter = u * horner(sin_terms, u * u)
        half = 1.0 - 0.5**0.5 * quarter * quarter
        y = d * ((radial_count - 1) / radius_cut) - float(middle)
        centre = half * half * mask * jnp.exp(-0.5 * y * y)
        ratio = jnp.exp(y)
        back = jnp.exp(-y)
        put(middle, centre.astype(jnp.bfloat16))
        value = centre
        for k in range(middle + 1, radial_count):
            value = value * ratio
            put(k, value.astype(jnp.bfloat16))
        value = centre
        for k in range(middle - 1, -1, -1):
            value = value * back
            put(k, value.astype(jnp.bfloat16))

    block_values = own_ref[:rows, :]

    def products(i):
        found = jnp.dot(tiles_ref[i % 2], block_values, preferred_element_type=jnp.float32)
        near_ref[i * step : (i + 1) * step, :] = weighted(found, step, filter_ref)

    for i in range(rows // step):
        for low in range(i * step, (i + 1) * step, part):
            inner = low - i * step

            def put(k, value):
                at = k * step + inner
                tiles_ref[i % 2, at : at + part, :] = value

            def put_far(column):
                def store(k, value):
                    at = k * rows + low
                    far_tiles_ref[at : at + part, column : column + rows] = value

                return store

            make(low, 1, put)
            make(low, sibling, put_far(0))
            make(low, 2 - sibling, put_far(rows))
        if i:
            products(i - 1)
    products(rows // step - 1)


def near_masks(blocks):
    return sorted({a ^ ((a + 1) % blocks) for a in range(blocks)})


def pick_kernel(*refs):
    own_ref, chunks, out_ref = refs[0], refs[1:-1], refs[-1]
    rows = out_ref.shape[0] // 2
    out_ref[:rows, :] = own_ref[:rows, :]
    blocks, block = lax.axis_size("atoms"), lax.axis_index("atoms")
    side = lax.rem(block + 1 - 2 * lax.axis_index("waves") + blocks, blocks)
    for mask, chunk in zip(near_masks(blocks), chunks):

        @pl.when((block ^ side) == mask)
        def _():
            out_ref[rows:, :] = chunk[:rows, :]


def beyond_kernel(
    scale,
    near_in_ref,
    far_tiles_ref,
    filter_ref,
    side_ref,
    features_ref,
    turned_ref,
    shared_ref,
    combined_ref,
):
    rows = near_in_ref.shape[0]
    found = jnp.dot(far_tiles_ref[...], side_ref[...], preferred_element_type=jnp.float32)
    far = jnp.dot(turned_ref[...], shared_ref[...], preferred_element_type=jnp.float32)
    combined_ref[...] = (
        features_ref[...].astype(jnp.float32)
        + near_in_ref[...]
        + weighted(found, rows, filter_ref)
        + far * scale
    )


def update_kernel(
    scale,
    count_ref,
    combined_ref,
    received_ref,
    turned_ref,
    gain_ref,
    w_inner_ref,
    w_outer_ref,
    out_ref,
):
    quarter = received_ref.shape[0] // 4
    received = jnp.concatenate(
        [received_ref[i * quarter : (i + 1) * quarter, :] for i in (1, 0, 3, 2)], axis=0
    )
    far = jnp.dot(turned_ref[...], received, preferred_element_type=jnp.float32)
    combined = combined_ref[...] + far * scale
    spread = lax.rsqrt(jnp.mean(combined * combined, axis=-1, keepdims=True) + 1e-06)
    normed = (combined * spread * gain_ref[...]).astype(jnp.bfloat16)
    inner = jnp.dot(normed, w_inner_ref[...], preferred_element_type=jnp.float32)
    inner = (inner / (1.0 + jnp.exp(-inner))).astype(jnp.bfloat16)
    result = jnp.dot(inner, w_outer_ref[...], preferred_element_type=jnp.float32)
    row = lax.broadcasted_iota(jnp.int32, result.shape, 0)
    out_ref[...] = jnp.where(row < count_ref[...].reshape(1, 1), result, 0.0).astype(jnp.bfloat16)


hbm = pl.BlockSpec(memory_space=pltpu.HBM)
vmem = pl.BlockSpec(memory_space=pltpu.VMEM)


def call(kernel, specs, outs, scratch=(), micros=1.0, mib=8, final=False):
    make = jax.ShapeDtypeStruct if final else pltpu.VMEM
    shapes = tuple(make(shape, dtype) for shape, dtype in outs)
    return pl.pallas_call(
        kernel,
        in_specs=specs,
        out_specs=tuple(vmem for _ in outs),
        out_shape=shapes,
        scratch_shapes=list(scratch),
        cost_estimate=pl.CostEstimate(
            flops=int(micros * 1.1e9), bytes_accessed=int(micros * 1e6), transcendentals=0
        ),
        compiler_params=pltpu.CompilerParams(vmem_limit_bytes=mib * 1024 * 1024),
    )


def gathered_parts(
    features,
    positions,
    distances,
    pair_mask,
    counts,
    wave_index,
    w_value,
    filter_short,
    filter_long,
    gain,
    w_inner,
    w_outer,
):
    rows, width = features.shape
    radial_count = filter_short.shape[0]
    wave_count = wave_index.shape[1]
    blocks, cores = lax.axis_size("atoms"), lax.axis_size("waves")
    bf16, f32 = jnp.bfloat16, jnp.float32

    def across(mask):
        return [
            (a * cores + c, (a ^ mask) * cores + c) for a in range(blocks) for c in range(cores)
        ]

    over = [(a * cores + c, a * cores + 1 - c) for a in range(blocks) for c in range(cores)]

    chunk_rows = rows + extra_rows
    (chunk,) = call(
        prepare_kernel,
        [hbm, hbm, hbm, hbm],
        [((chunk_rows, width), bf16)],
        [
            pltpu.VMEM(features.shape, features.dtype),
            pltpu.VMEM(w_value.shape, w_value.dtype),
            pltpu.VMEM(positions.shape, positions.dtype),
            pltpu.SMEM(counts.shape, counts.dtype),
            pltpu.SemaphoreType.DMA((4,)),
        ],
        micros=6.0,
        mib=60,
    )(features, w_value, positions, counts)

    def move(value, mask):
        return lax.ppermute(value, both, across(mask))

    def swap(value):
        return lax.ppermute(value, both, over)

    starts, passed = move_masks(blocks)
    got = {0: chunk, **{mask: move(chunk, mask) for mask in starts}}
    for mask in passed:
        got[mask] = lax.ppermute(got[starts[0]], both, across(starts[0] ^ mask))
    other_waves = swap(wave_index)

    wave_total = wave_count * cores
    sums_shape = ((2 * wave_total, width), f32)
    waves, wave_weights = call(
        functools.partial(waves_kernel, float(rows * blocks * cores) ** -0.5),
        [vmem] * 3,
        [((wave_total, extra_rows), bf16), ((wave_total, width), f32)],
        micros=1.0,
    )(wave_index, other_waves, filter_long)
    step = rows // 4
    near, far_tiles = call(
        functools.partial(near_kernel, step=step),
        [vmem] * 4,
        [((rows, width), f32), ((radial_count * rows, 2 * rows), bf16)],
        [pltpu.VMEM((2, radial_count * step, rows), bf16)],
        micros=2.5,
        mib=16,
    )(distances, pair_mask, filter_short, chunk)

    first, last = sum_groups(blocks)
    sums, turned = call(
        first_kernel,
        [vmem] * (1 + len(first)),
        [sums_shape, ((rows, 2 * wave_total), bf16)],
        [phase_scratch(len(first), rows)],
        micros=0.9 * len(first),
        mib=12,
    )(waves, *(got[mask] for mask in first))
    (side,) = call(
        pick_kernel, [vmem] * (1 + len(near_masks(blocks))), [((2 * rows, width), bf16)], micros=0.3
    )(chunk, *(got[mask] for mask in near_masks(blocks)))
    side = swap(side)
    (shared,) = call(
        last_kernel,
        [vmem] * (3 + len(last)),
        [(sums_shape[0], bf16)],
        [phase_scratch(len(last), rows), pltpu.VMEM(sums_shape[0], f32)],
        micros=0.9 * len(last),
        mib=12,
    )(waves, sums, wave_weights, *(got[mask] for mask in last))
    received = swap(shared)
    scale = float(wave_total) ** -0.5
    (combined,) = call(
        functools.partial(beyond_kernel, scale),
        [vmem] * 7,
        [((rows, width), f32)],
        micros=1.5,
        mib=12,
    )(near, far_tiles, filter_short, side, features, turned, shared)
    return call(
        functools.partial(update_kernel, scale),
        [vmem] * 7,
        [((rows, width), bf16)],
        micros=1.0,
        final=True,
    )(counts, combined, received, turned, jnp.reshape(gain, (1, width)), w_inner, w_outer)[0]


def phase_scratch(chunks, rows, block=128):
    return pltpu.VMEM((2, 2 * block, chunks * rows), jnp.bfloat16)


def gathered_body(*args):
    return gathered_parts(*args)


def move_masks(blocks):
    half = blocks // 2
    direct = list(range(half - 1, 0, -1))
    return [half] + direct, [half ^ mask for mask in direct]


def sum_groups(blocks):
    starts, passed = move_masks(blocks)
    return [0] + starts[1:] + starts[:1], passed


def gathers(mesh):
    blocks, cores = mesh.shape["atoms"], mesh.shape["waves"]
    return cores == 2 and 4 <= blocks <= gather_limit and blocks & (blocks - 1) == 0


def solution(mesh):
    placed = (
        P(("groups", "atoms", "waves"), None),
        P(None, ("groups", "atoms", "waves")),
        P(("groups", "atoms", "waves"), None),
        P(("groups", "atoms", "waves"), None),
        P(("groups", "atoms", "waves")),
        P(None, ("groups", "waves")),
        P(),
        P(),
        P(),
        P(),
        P(),
        P(),
    )
    mapped = jax.shard_map(
        gathered_body if gathers(mesh) else summed_body,
        mesh=mesh,
        in_specs=placed,
        out_specs=P(("groups", "atoms", "waves"), None),
        check_vma=False,
    )
    return mapped if gathers(mesh) else mapped
```

```python
import functools
import math

import jax
import jax.numpy as jnp
from jax import lax
from jax.experimental import pallas as pl
from jax.experimental.pallas import tpu as pltpu
from jax.sharding import PartitionSpec as P

radius_cut = 5.0
wave_top = 6.0 * 3.0**0.5
both = ("atoms", "waves")
gather_limit = 8
extra_rows = 16

sin_terms = (2.641737538071335, -1.0859062893731768, 0.13047468843565363)


def padded(block, sides, width):
    for axis, dim in sides:
        count = lax.axis_size(axis)
        forward = [(i, i + 1) for i in range(count - 1)]
        forward.append((count - 1, 0))
        backward = [(target, source) for source, target in forward]
        low = lax.ppermute(
            lax.slice_in_dim(block, block.shape[dim] - width, None, axis=dim), axis, forward
        )
        high = lax.ppermute(lax.slice_in_dim(block, 0, width, axis=dim), axis, backward)
        block = jnp.concatenate([low, block, high], axis=dim)
    return block


def radial_tiles(distances, pair_mask, radial_count):
    centres = radius_cut * jnp.arange(radial_count, dtype=jnp.float32) / (radial_count - 1)
    spacing = radius_cut / (radial_count - 1)
    envelope = (
        0.5 * (jnp.cos(jnp.pi * distances / radius_cut) + 1.0) * pair_mask.astype(jnp.float32)
    )
    offsets = (distances[None] - centres[:, None, None]) / spacing
    tiles = jnp.exp(-0.5 * offsets * offsets) * envelope[None]
    return tiles.astype(jnp.bfloat16)


def phase_tiles(points, wave_index):
    waves = wave_index.astype(jnp.float32)
    theta = points[0][:, None] * waves[0][None, :] + points[1][:, None] * waves[1][None, :]
    theta = 2.0 * jnp.pi * (theta + points[2][:, None] * waves[2][None, :])
    return (jnp.cos(theta).astype(jnp.bfloat16), jnp.sin(theta).astype(jnp.bfloat16))


def wave_filter(wave_index, filter_long):
    waves = wave_index.astype(jnp.float32)
    radial_count = filter_long.shape[0]
    magnitude = jnp.sqrt(waves[0] * waves[0] + waves[1] * waves[1] + waves[2] * waves[2])
    centres = wave_top * jnp.arange(radial_count, dtype=jnp.float32) / (radial_count - 1)
    spacing = wave_top / (radial_count - 1)
    offsets = (magnitude[None, :] - centres[:, None]) / spacing
    k_basis = jnp.exp(-0.5 * offsets * offsets)
    return jnp.dot(k_basis.T, filter_long, precision=lax.Precision.HIGHEST)


def summed_body(
    features,
    positions,
    distances,
    pair_mask,
    counts,
    wave_index,
    w_value,
    filter_short,
    filter_long,
    gain,
    w_inner,
    w_outer,
):
    row_count = features.shape[0]
    width = features.shape[1]
    radial_count = filter_short.shape[0]
    occupied = (lax.iota(jnp.int32, row_count) < counts[0]).astype(jnp.float32)
    values = (
        jnp.dot(features, w_value, preferred_element_type=jnp.float32) * occupied[:, None]
    ).astype(jnp.bfloat16)
    beside_all = padded(values, ((("atoms", "waves"), 0),), row_count)
    tiles = radial_tiles(distances, pair_mask, radial_count).reshape(
        radial_count * row_count, 3 * row_count
    )
    products = jnp.dot(tiles, beside_all, preferred_element_type=jnp.float32).reshape(
        radial_count, row_count, width
    )
    near_field = jnp.sum(products * filter_short[:, None, :], axis=0)
    wide_values, block_points = (
        lax.all_gather(values.astype(jnp.float32), "waves", axis=0, tiled=True),
        lax.all_gather(positions, "waves", axis=1, tiled=True),
    )
    block_values = wide_values.astype(jnp.bfloat16)
    cosine, sine = phase_tiles(block_points, wave_index)
    cos_sum = jnp.einsum("ak,af->kf", cosine, block_values, preferred_element_type=jnp.float32)
    sin_sum = jnp.einsum("ak,af->kf", sine, block_values, preferred_element_type=jnp.float32)
    atom_total = row_count * lax.axis_size(("atoms", "waves"))
    wave_total = wave_index.shape[1] * lax.axis_size("waves")
    factor_scale = float(atom_total) ** (-0.5)
    cos_total, sin_total = lax.psum((cos_sum, sin_sum), "atoms")
    block_filter = wave_filter(wave_index, filter_long)
    cos_filtered = (cos_total * block_filter * factor_scale).astype(jnp.bfloat16)
    sin_filtered = (sin_total * block_filter * factor_scale).astype(jnp.bfloat16)
    far_field = lax.psum_scatter(
        (
            jnp.dot(cosine, cos_filtered, preferred_element_type=jnp.float32)
            + jnp.dot(sine, sin_filtered, preferred_element_type=jnp.float32)
        ).astype(jnp.bfloat16),
        "waves",
        scatter_dimension=0,
        tiled=True,
    ).astype(jnp.float32) * float(wave_total) ** (-0.5)
    combined = features.astype(jnp.float32) + near_field + far_field
    normed = (
        combined * lax.rsqrt(jnp.mean(combined * combined, axis=-1, keepdims=True) + 1e-06) * gain
    ).astype(jnp.bfloat16)
    inner = jax.nn.silu(jnp.dot(normed, w_inner, preferred_element_type=jnp.float32)).astype(
        jnp.bfloat16
    )
    result = jnp.dot(inner, w_outer, preferred_element_type=jnp.float32) * occupied[:, None]
    return result.astype(jnp.bfloat16)


def horner(terms, w):
    total = jnp.full_like(w, terms[-1])
    for term in terms[-2::-1]:
        total = total * w + term
    return total


def phases(turns):
    r = turns - jnp.round(turns)
    quarter = r * horner(sin_terms, r * r)
    square = quarter * quarter
    rest = 2.0**1.5 - square
    half_sin = quarter * (rest * lax.rsqrt(rest))
    half_cos = 2.0**0.5 - square
    return 1.0 - half_sin * half_sin, half_sin * half_cos


def add_sums(sums_in, sums_ref, chunks, wave_ref, phase_ref, turned_ref=None, step=64):
    rows = chunks[0].shape[0] - extra_rows
    wave_count = wave_ref.shape[0]
    block = wave_count // phase_ref.shape[0]
    block_values = [chunk[:rows, :] for chunk in chunks]
    block_values = jnp.concatenate(block_values, axis=0) if len(chunks) > 1 else block_values[0]
    for index, start in enumerate(range(0, wave_count, block)):
        slot = phase_ref.at[index]
        for i, chunk in enumerate(chunks):
            part = slice(i * rows, (i + 1) * rows)
            for low in range(0, block, step):
                turns = jnp.dot(
                    wave_ref[start + low : start + low + step, :],
                    chunk[rows:, :],
                    preferred_element_type=jnp.float32,
                )
                cosine, sine = phases(turns)
                slot[low : low + step, part] = cosine.astype(jnp.bfloat16)
                slot[block + low : block + low + step, part] = sine.astype(jnp.bfloat16)
        found = jnp.dot(slot[...], block_values, preferred_element_type=jnp.float32)
        for first, rank in ((start, 0), (wave_count + start, block)):
            value = found[rank : rank + block, :]
            if sums_in is not None:
                value = sums_in[first : first + block, :] + value
            sums_ref[first : first + block, :] = value
            if turned_ref is not None:
                turned_ref[:, first : first + block] = slot[rank : rank + block, :rows].T


def fetch(sources, targets, semaphores):
    copies = [
        pltpu.make_async_copy(source, target, semaphores.at[i])
        for i, (source, target) in enumerate(zip(sources, targets))
    ]
    for copy in copies:
        copy.start()
    for copy in copies:
        copy.wait()


def pieces(value):
    high = value.astype(jnp.bfloat16).astype(jnp.float32)
    middle = (value - high).astype(jnp.bfloat16).astype(jnp.float32)
    return high, middle, value - high - middle


def prepare_kernel(
    features_hbm,
    w_value_hbm,
    positions_hbm,
    count_hbm,
    chunk_ref,
    features,
    w_value,
    positions,
    count_ref,
    sems,
):
    fetch(
        (features_hbm, w_value_hbm, positions_hbm, count_hbm),
        (features, w_value, positions, count_ref),
        sems,
    )
    rows = features.shape[0]
    values = jnp.dot(features[...], w_value[...], preferred_element_type=jnp.float32)
    row = lax.broadcasted_iota(jnp.int32, values.shape, 0)
    chunk_ref[:rows, :] = jnp.where(row < count_ref[0], values, 0.0).astype(jnp.bfloat16)
    points = positions[...]
    high, middle, low = pieces(points)
    spare = jnp.zeros((extra_rows - 9, rows), jnp.float32)
    chunk_ref[rows:, :] = jnp.concatenate([high, middle, low, spare], axis=0).astype(jnp.bfloat16)


def waves_kernel(
    scale, own_wave_ref, other_wave_ref, filter_long_ref, waves_ref, weights_ref
):
    waves = jnp.concatenate([own_wave_ref[...], other_wave_ref[...]], axis=1).astype(jnp.float32)
    spare = jnp.zeros((extra_rows - 9, waves.shape[1]), jnp.float32)
    waves_ref[...] = jnp.concatenate([waves, waves, waves, spare], axis=0).T.astype(jnp.bfloat16)
    radial_count = filter_long_ref.shape[0]
    magnitude = jnp.sqrt(
        waves[0:1] * waves[0:1] + waves[1:2] * waves[1:2] + waves[2:3] * waves[2:3]
    )
    spacing = wave_top / (radial_count - 1)
    index = lax.broadcasted_iota(jnp.int32, (radial_count, waves.shape[1]), 0)
    offsets = magnitude / spacing - index.astype(jnp.float32)
    basis = jnp.exp(-0.5 * offsets * offsets)
    high, middle, low = pieces(basis)
    rows = jnp.concatenate([high, high, middle, high, low, middle], axis=0)
    high, middle, low = pieces(filter_long_ref[...])
    columns = jnp.concatenate([high, middle, high, low, high, middle], axis=0)
    weights_ref[...] = scale * jnp.dot(
        rows.T.astype(jnp.bfloat16),
        columns.astype(jnp.bfloat16),
        preferred_element_type=jnp.float32,
    )


def first_kernel(wave_ref, *refs):
    chunks, (sums_ref, turned_ref, phase_ref) = refs[:-3], refs[-3:]
    add_sums(None, sums_ref, chunks, wave_ref, phase_ref, turned_ref)


def more_kernel(wave_ref, sums_in_ref, *refs):
    chunks, (sums_ref, phase_ref) = refs[:-2], refs[-2:]
    add_sums(sums_in_ref, sums_ref, chunks, wave_ref, phase_ref)


def last_kernel(wave_ref, sums_in_ref, weights_ref, *refs):
    chunks, (shared_ref, phase_ref, sums_ref) = refs[:-3], refs[-3:]
    add_sums(sums_in_ref, sums_ref, chunks, wave_ref, phase_ref)
    wave_count = wave_ref.shape[0]
    for start in (0, wave_count):
        part = slice(start, start + wave_count)
        shared_ref[part, :] = (sums_ref[part, :] * weights_ref[...]).astype(jnp.bfloat16)


def weighted(products, rows, filter_ref):
    radial_count = filter_ref.shape[0]
    total = None
    for k in range(radial_count):
        m = k - radial_count // 2
        term = products[k * rows : (k + 1) * rows, :] * (
            filter_ref[k : k + 1, :] * math.exp(-0.5 * m * m)
        )
        total = term if total is None else total + term
    return total


def near_kernel(
    distances_ref,
    mask_ref,
    filter_ref,
    own_ref,
    near_ref,
    far_tiles_ref,
    tiles_ref,
    *,
    step,
    part=32,
):
    rows = distances_ref.shape[0]
    radial_count = filter_ref.shape[0]
    middle = radial_count // 2
    sibling = 2 - 2 * lax.axis_index("waves")

    def make(low, block, put):
        start = block * rows if isinstance(block, int) else pl.multiple_of(block * rows, rows)
        d = distances_ref[low : low + part, pl.ds(start, rows)]
        mask = mask_ref[low : low + part, pl.ds(start, rows)].astype(jnp.float32)
        u = d * (0.5 / radius_cut)
        quarter = u * horner(sin_terms, u * u)
        half = 1.0 - 0.5**0.5 * quarter * quarter
        y = d * ((radial_count - 1) / radius_cut) - float(middle)
        centre = half * half * mask * jnp.exp(-0.5 * y * y)
        ratio = jnp.exp(y)
        back = jnp.exp(-y)
        put(middle, centre.astype(jnp.bfloat16))
        value = centre
        for k in range(middle + 1, radial_count):
            value = value * ratio
            put(k, value.astype(jnp.bfloat16))
        value = centre
        for k in range(middle - 1, -1, -1):
            value = value * back
            put(k, value.astype(jnp.bfloat16))

    block_values = own_ref[:rows, :]

    def products(i):
        found = jnp.dot(tiles_ref[i % 2], block_values, preferred_element_type=jnp.float32)
        near_ref[i * step : (i + 1) * step, :] = weighted(found, step, filter_ref)

    for i in range(rows // step):
        for low in range(i * step, (i + 1) * step, part):
            inner = low - i * step

            def put(k, value):
                at = k * step + inner
                tiles_ref[i % 2, at : at + part, :] = value

            def put_far(column):
                def store(k, value):
                    at = k * rows + low
                    far_tiles_ref[at : at + part, column : column + rows] = value

                return store

            make(low, 1, put)
            make(low, sibling, put_far(0))
            make(low, 2 - sibling, put_far(rows))
        if i:
            products(i - 1)
    products(rows // step - 1)


def near_masks(blocks):
    return sorted({a ^ ((a + 1) % blocks) for a in range(blocks)})


def pick_kernel(*refs):
    own_ref, chunks, out_ref = refs[0], refs[1:-1], refs[-1]
    rows = out_ref.shape[0] // 2
    out_ref[:rows, :] = own_ref[:rows, :]
    blocks, block = lax.axis_size("atoms"), lax.axis_index("atoms")
    side = lax.rem(block + 1 - 2 * lax.axis_index("waves") + blocks, blocks)
    for mask, chunk in zip(near_masks(blocks), chunks):

        @pl.when((block ^ side) == mask)
        def _():
            out_ref[rows:, :] = chunk[:rows, :]


def beyond_kernel(
    scale,
    near_in_ref,
    far_tiles_ref,
    filter_ref,
    side_ref,
    features_ref,
    turned_ref,
    shared_ref,
    combined_ref,
):
    rows = near_in_ref.shape[0]
    found = jnp.dot(far_tiles_ref[...], side_ref[...], preferred_element_type=jnp.float32)
    far = jnp.dot(turned_ref[...], shared_ref[...], preferred_element_type=jnp.float32)
    combined_ref[...] = (
        features_ref[...].astype(jnp.float32)
        + near_in_ref[...]
        + weighted(found, rows, filter_ref)
        + far * scale
    )


def update_kernel(
    scale,
    count_ref,
    combined_ref,
    received_ref,
    turned_ref,
    gain_ref,
    w_inner_ref,
    w_outer_ref,
    out_ref,
):
    quarter = received_ref.shape[0] // 4
    received = jnp.concatenate(
        [received_ref[i * quarter : (i + 1) * quarter, :] for i in (1, 0, 3, 2)], axis=0
    )
    far = jnp.dot(turned_ref[...], received, preferred_element_type=jnp.float32)
    combined = combined_ref[...] + far * scale
    spread = lax.rsqrt(jnp.mean(combined * combined, axis=-1, keepdims=True) + 1e-06)
    normed = (combined * spread * gain_ref[...]).astype(jnp.bfloat16)
    inner = jnp.dot(normed, w_inner_ref[...], preferred_element_type=jnp.float32)
    inner = (inner / (1.0 + jnp.exp(-inner))).astype(jnp.bfloat16)
    result = jnp.dot(inner, w_outer_ref[...], preferred_element_type=jnp.float32)
    row = lax.broadcasted_iota(jnp.int32, result.shape, 0)
    out_ref[...] = jnp.where(row < count_ref[...].reshape(1, 1), result, 0.0).astype(jnp.bfloat16)


hbm = pl.BlockSpec(memory_space=pltpu.HBM)
vmem = pl.BlockSpec(memory_space=pltpu.VMEM)


def call(kernel, specs, outs, scratch=(), micros=1.0, mib=8, final=False):
    make = jax.ShapeDtypeStruct if final else pltpu.VMEM
    shapes = tuple(make(shape, dtype) for shape, dtype in outs)
    return pl.pallas_call(
        kernel,
        in_specs=specs,
        out_specs=tuple(vmem for _ in outs),
        out_shape=shapes,
        scratch_shapes=list(scratch),
        cost_estimate=pl.CostEstimate(
            flops=int(micros * 1.1e9), bytes_accessed=int(micros * 1e6), transcendentals=0
        ),
        compiler_params=pltpu.CompilerParams(vmem_limit_bytes=mib * 1024 * 1024),
    )


def gathered_parts(
    features,
    positions,
    distances,
    pair_mask,
    counts,
    wave_index,
    w_value,
    filter_short,
    filter_long,
    gain,
    w_inner,
    w_outer,
):
    rows, width = features.shape
    radial_count = filter_short.shape[0]
    wave_count = wave_index.shape[1]
    blocks, cores = lax.axis_size("atoms"), lax.axis_size("waves")
    bf16, f32 = jnp.bfloat16, jnp.float32

    def across(mask):
        return [
            (a * cores + c, (a ^ mask) * cores + c) for a in range(blocks) for c in range(cores)
        ]

    over = [(a * cores + c, a * cores + 1 - c) for a in range(blocks) for c in range(cores)]

    chunk_rows = rows + extra_rows
    (chunk,) = call(
        prepare_kernel,
        [hbm, hbm, hbm, hbm],
        [((chunk_rows, width), bf16)],
        [
            pltpu.VMEM(features.shape, features.dtype),
            pltpu.VMEM(w_value.shape, w_value.dtype),
            pltpu.VMEM(positions.shape, positions.dtype),
            pltpu.SMEM(counts.shape, counts.dtype),
            pltpu.SemaphoreType.DMA((4,)),
        ],
        micros=6.0,
        mib=60,
    )(features, w_value, positions, counts)

    def move(value, mask):
        return lax.ppermute(value, both, across(mask))

    def swap(value):
        return lax.ppermute(value, both, over)

    starts, passed = move_masks(blocks)
    got = {0: chunk, **{mask: move(chunk, mask) for mask in starts}}
    for mask in passed:
        got[mask] = lax.ppermute(got[starts[0]], both, across(starts[0] ^ mask))
    other_waves = swap(wave_index)

    wave_total = wave_count * cores
    sums_shape = ((2 * wave_total, width), f32)
    waves, wave_weights = call(
        functools.partial(waves_kernel, float(rows * blocks * cores) ** -0.5),
        [vmem] * 3,
        [((wave_total, extra_rows), bf16), ((wave_total, width), f32)],
        micros=1.0,
    )(wave_index, other_waves, filter_long)
    step = rows // 4
    near, far_tiles = call(
        functools.partial(near_kernel, step=step),
        [vmem] * 4,
        [((rows, width), f32), ((radial_count * rows, 2 * rows), bf16)],
        [pltpu.VMEM((2, radial_count * step, rows), bf16)],
        micros=2.5,
        mib=16,
    )(distances, pair_mask, filter_short, chunk)

    first, *later, last = sum_groups(blocks)
    sums, turned = call(
        first_kernel,
        [vmem] * (1 + len(first)),
        [sums_shape, ((rows, 2 * wave_total), bf16)],
        [phase_scratch(len(first), rows, wave_total)],
        micros=0.9 * len(first),
        mib=12,
    )(waves, *(got[mask] for mask in first))
    (side,) = call(
        pick_kernel, [vmem] * (1 + len(near_masks(blocks))), [((2 * rows, width), bf16)], micros=0.3
    )(chunk, *(got[mask] for mask in near_masks(blocks)))
    side = swap(side)
    for masks in later:
        (sums,) = call(
            more_kernel,
            [vmem] * (2 + len(masks)),
            [sums_shape],
            [phase_scratch(len(masks), rows, wave_total)],
            micros=0.9 * len(masks),
            mib=12,
        )(waves, sums, *(got[mask] for mask in masks))
    (shared,) = call(
        last_kernel,
        [vmem] * (3 + len(last)),
        [(sums_shape[0], bf16)],
        [phase_scratch(len(last), rows, wave_total), pltpu.VMEM(sums_shape[0], f32)],
        micros=0.9 * len(last),
        mib=12,
    )(waves, sums, wave_weights, *(got[mask] for mask in last))
    received = swap(shared)
    scale = float(wave_total) ** -0.5
    (combined,) = call(
        functools.partial(beyond_kernel, scale),
        [vmem] * 7,
        [((rows, width), f32)],
        micros=1.5,
        mib=12,
    )(near, far_tiles, filter_short, side, features, turned, shared)
    return call(
        functools.partial(update_kernel, scale),
        [vmem] * 7,
        [((rows, width), bf16)],
        micros=1.0,
        final=True,
    )(counts, combined, received, turned, jnp.reshape(gain, (1, width)), w_inner, w_outer)[0]


def phase_scratch(chunks, rows, waves, blocks=2):
    return pltpu.VMEM((blocks, 2 * waves // blocks, chunks * rows), jnp.bfloat16)


def gathered_body(*args):
    return gathered_parts(*args)


def move_masks(blocks):
    half = blocks // 2
    direct = list(range(half - 1, 0, -1))
    return [half] + direct, [half ^ mask for mask in direct]


def sum_groups(blocks):
    starts, passed = move_masks(blocks)
    groups = [[0] + starts[-1:] + starts[:1], starts[1:-1], passed[:1], passed[1:]]
    return [group for group in groups if group]


def gathers(mesh):
    blocks, cores = mesh.shape["atoms"], mesh.shape["waves"]
    return cores == 2 and 4 <= blocks <= gather_limit and blocks & (blocks - 1) == 0


def solution(mesh):
    placed = (
        P(("groups", "atoms", "waves"), None),
        P(None, ("groups", "atoms", "waves")),
        P(("groups", "atoms", "waves"), None),
        P(("groups", "atoms", "waves"), None),
        P(("groups", "atoms", "waves")),
        P(None, ("groups", "waves")),
        P(),
        P(),
        P(),
        P(),
        P(),
        P(),
    )
    mapped = jax.shard_map(
        gathered_body if gathers(mesh) else summed_body,
        mesh=mesh,
        in_specs=placed,
        out_specs=P(("groups", "atoms", "waves"), None),
        check_vma=False,
    )
    return mapped if gathers(mesh) else mapped
```

```python
import functools
import math

import jax
import jax.numpy as jnp
from jax import lax
from jax.experimental import pallas as pl
from jax.experimental.pallas import tpu as pltpu
from jax.sharding import PartitionSpec as P

radius_cut = 5.0
wave_top = 6.0 * 3.0**0.5
both = ("atoms", "waves")
gather_limit = 8
extra_rows = 16

sin_terms = (2.641737538071335, -1.0859062893731768, 0.13047468843565363)


def padded(block, sides, width):
    for axis, dim in sides:
        count = lax.axis_size(axis)
        forward = [(i, i + 1) for i in range(count - 1)]
        forward.append((count - 1, 0))
        backward = [(target, source) for source, target in forward]
        low = lax.ppermute(
            lax.slice_in_dim(block, block.shape[dim] - width, None, axis=dim), axis, forward
        )
        high = lax.ppermute(lax.slice_in_dim(block, 0, width, axis=dim), axis, backward)
        block = jnp.concatenate([low, block, high], axis=dim)
    return block


def radial_tiles(distances, pair_mask, radial_count):
    centres = radius_cut * jnp.arange(radial_count, dtype=jnp.float32) / (radial_count - 1)
    spacing = radius_cut / (radial_count - 1)
    envelope = (
        0.5 * (jnp.cos(jnp.pi * distances / radius_cut) + 1.0) * pair_mask.astype(jnp.float32)
    )
    offsets = (distances[None] - centres[:, None, None]) / spacing
    tiles = jnp.exp(-0.5 * offsets * offsets) * envelope[None]
    return tiles.astype(jnp.bfloat16)


def phase_tiles(points, wave_index):
    waves = wave_index.astype(jnp.float32)
    theta = points[0][:, None] * waves[0][None, :] + points[1][:, None] * waves[1][None, :]
    theta = 2.0 * jnp.pi * (theta + points[2][:, None] * waves[2][None, :])
    return (jnp.cos(theta).astype(jnp.bfloat16), jnp.sin(theta).astype(jnp.bfloat16))


def wave_filter(wave_index, filter_long):
    waves = wave_index.astype(jnp.float32)
    radial_count = filter_long.shape[0]
    magnitude = jnp.sqrt(waves[0] * waves[0] + waves[1] * waves[1] + waves[2] * waves[2])
    centres = wave_top * jnp.arange(radial_count, dtype=jnp.float32) / (radial_count - 1)
    spacing = wave_top / (radial_count - 1)
    offsets = (magnitude[None, :] - centres[:, None]) / spacing
    k_basis = jnp.exp(-0.5 * offsets * offsets)
    return jnp.dot(k_basis.T, filter_long, precision=lax.Precision.HIGHEST)


def summed_body(
    features,
    positions,
    distances,
    pair_mask,
    counts,
    wave_index,
    w_value,
    filter_short,
    filter_long,
    gain,
    w_inner,
    w_outer,
):
    row_count = features.shape[0]
    width = features.shape[1]
    radial_count = filter_short.shape[0]
    occupied = (lax.iota(jnp.int32, row_count) < counts[0]).astype(jnp.float32)
    values = (
        jnp.dot(features, w_value, preferred_element_type=jnp.float32) * occupied[:, None]
    ).astype(jnp.bfloat16)
    beside_all = padded(values, ((("atoms", "waves"), 0),), row_count)
    tiles = radial_tiles(distances, pair_mask, radial_count).reshape(
        radial_count * row_count, 3 * row_count
    )
    products = jnp.dot(tiles, beside_all, preferred_element_type=jnp.float32).reshape(
        radial_count, row_count, width
    )
    near_field = jnp.sum(products * filter_short[:, None, :], axis=0)
    wide_values, block_points = (
        lax.all_gather(values.astype(jnp.float32), "waves", axis=0, tiled=True),
        lax.all_gather(positions, "waves", axis=1, tiled=True),
    )
    block_values = wide_values.astype(jnp.bfloat16)
    cosine, sine = phase_tiles(block_points, wave_index)
    cos_sum = jnp.einsum("ak,af->kf", cosine, block_values, preferred_element_type=jnp.float32)
    sin_sum = jnp.einsum("ak,af->kf", sine, block_values, preferred_element_type=jnp.float32)
    atom_total = row_count * lax.axis_size(("atoms", "waves"))
    wave_total = wave_index.shape[1] * lax.axis_size("waves")
    factor_scale = float(atom_total) ** (-0.5)
    cos_total, sin_total = lax.psum((cos_sum, sin_sum), "atoms")
    block_filter = wave_filter(wave_index, filter_long)
    cos_filtered = (cos_total * block_filter * factor_scale).astype(jnp.bfloat16)
    sin_filtered = (sin_total * block_filter * factor_scale).astype(jnp.bfloat16)
    far_field = lax.psum_scatter(
        (
            jnp.dot(cosine, cos_filtered, preferred_element_type=jnp.float32)
            + jnp.dot(sine, sin_filtered, preferred_element_type=jnp.float32)
        ).astype(jnp.bfloat16),
        "waves",
        scatter_dimension=0,
        tiled=True,
    ).astype(jnp.float32) * float(wave_total) ** (-0.5)
    combined = features.astype(jnp.float32) + near_field + far_field
    normed = (
        combined * lax.rsqrt(jnp.mean(combined * combined, axis=-1, keepdims=True) + 1e-06) * gain
    ).astype(jnp.bfloat16)
    inner = jax.nn.silu(jnp.dot(normed, w_inner, preferred_element_type=jnp.float32)).astype(
        jnp.bfloat16
    )
    result = jnp.dot(inner, w_outer, preferred_element_type=jnp.float32) * occupied[:, None]
    return result.astype(jnp.bfloat16)


def horner(terms, w):
    total = jnp.full_like(w, terms[-1])
    for term in terms[-2::-1]:
        total = total * w + term
    return total


def phases(turns):
    r = turns - jnp.round(turns)
    quarter = r * horner(sin_terms, r * r)
    square = quarter * quarter
    rest = 2.0**1.5 - square
    half_sin = quarter * (rest * lax.rsqrt(rest))
    half_cos = 2.0**0.5 - square
    return 1.0 - half_sin * half_sin, half_sin * half_cos


def add_sums(sums_in, sums_ref, chunks, wave_ref, phase_ref, turned_ref=None, step=64):
    rows = chunks[0].shape[0] - extra_rows
    wave_count = wave_ref.shape[0]
    block = wave_count // phase_ref.shape[0]
    block_values = [chunk[:rows, :] for chunk in chunks]
    block_values = jnp.concatenate(block_values, axis=0) if len(chunks) > 1 else block_values[0]
    for index, start in enumerate(range(0, wave_count, block)):
        slot = phase_ref.at[index]
        for i, chunk in enumerate(chunks):
            part = slice(i * rows, (i + 1) * rows)
            for low in range(0, block, step):
                turns = jnp.dot(
                    wave_ref[start + low : start + low + step, :],
                    chunk[rows:, :],
                    preferred_element_type=jnp.float32,
                )
                cosine, sine = phases(turns)
                slot[low : low + step, part] = cosine.astype(jnp.bfloat16)
                slot[block + low : block + low + step, part] = sine.astype(jnp.bfloat16)
        found = jnp.dot(slot[...], block_values, preferred_element_type=jnp.float32)
        for first, rank in ((start, 0), (wave_count + start, block)):
            value = found[rank : rank + block, :]
            if sums_in is not None:
                value = sums_in[first : first + block, :] + value
            sums_ref[first : first + block, :] = value
            if turned_ref is not None:
                turned_ref[:, first : first + block] = slot[rank : rank + block, :rows].T


def pieces(value):
    high = value.astype(jnp.bfloat16).astype(jnp.float32)
    middle = (value - high).astype(jnp.bfloat16).astype(jnp.float32)
    return high, middle, value - high - middle


def blank_kernel(blank_ref):
    blank_ref[...] = jnp.zeros(blank_ref.shape, blank_ref.dtype)


def count_kernel(count_ref, blank_ref, held_ref):
    held_ref[...] = blank_ref[...] + count_ref[0]


def prepare_kernel(count_ref, features, w_value, positions, chunk_ref):
    rows = features.shape[0]
    values = jnp.dot(features[...], w_value[...], preferred_element_type=jnp.float32)
    row = lax.broadcasted_iota(jnp.int32, values.shape, 0)
    chunk_ref[:rows, :] = jnp.where(row < count_ref[:1, :1], values, 0.0).astype(jnp.bfloat16)
    points = positions[...]
    high, middle, low = pieces(points)
    spare = jnp.zeros((extra_rows - 9, rows), jnp.float32)
    chunk_ref[rows:, :] = jnp.concatenate([high, middle, low, spare], axis=0).astype(jnp.bfloat16)


def waves_kernel(
    scale, own_wave_ref, other_wave_ref, filter_long_ref, waves_ref, weights_ref
):
    waves = jnp.concatenate([own_wave_ref[...], other_wave_ref[...]], axis=1).astype(jnp.float32)
    spare = jnp.zeros((extra_rows - 9, waves.shape[1]), jnp.float32)
    waves_ref[...] = jnp.concatenate([waves, waves, waves, spare], axis=0).T.astype(jnp.bfloat16)
    radial_count = filter_long_ref.shape[0]
    magnitude = jnp.sqrt(
        waves[0:1] * waves[0:1] + waves[1:2] * waves[1:2] + waves[2:3] * waves[2:3]
    )
    spacing = wave_top / (radial_count - 1)
    index = lax.broadcasted_iota(jnp.int32, (radial_count, waves.shape[1]), 0)
    offsets = magnitude / spacing - index.astype(jnp.float32)
    basis = jnp.exp(-0.5 * offsets * offsets)
    high, middle, low = pieces(basis)
    rows = jnp.concatenate([high, high, middle, high, low, middle], axis=0)
    high, middle, low = pieces(filter_long_ref[...])
    columns = jnp.concatenate([high, middle, high, low, high, middle], axis=0)
    weights_ref[...] = scale * jnp.dot(
        rows.T.astype(jnp.bfloat16),
        columns.astype(jnp.bfloat16),
        preferred_element_type=jnp.float32,
    )


def first_kernel(wave_ref, *refs):
    chunks, (sums_ref, turned_ref, phase_ref) = refs[:-3], refs[-3:]
    add_sums(None, sums_ref, chunks, wave_ref, phase_ref, turned_ref)


def more_kernel(wave_ref, sums_in_ref, *refs):
    chunks, (sums_ref, phase_ref) = refs[:-2], refs[-2:]
    add_sums(sums_in_ref, sums_ref, chunks, wave_ref, phase_ref)


def last_kernel(wave_ref, sums_in_ref, weights_ref, *refs):
    chunks, (shared_ref, phase_ref, sums_ref) = refs[:-3], refs[-3:]
    add_sums(sums_in_ref, sums_ref, chunks, wave_ref, phase_ref)
    wave_count = wave_ref.shape[0]
    for start in (0, wave_count):
        part = slice(start, start + wave_count)
        shared_ref[part, :] = (sums_ref[part, :] * weights_ref[...]).astype(jnp.bfloat16)


def weighted(products, rows, filter_ref):
    radial_count = filter_ref.shape[0]
    total = None
    for k in range(radial_count):
        m = k - radial_count // 2
        term = products[k * rows : (k + 1) * rows, :] * (
            filter_ref[k : k + 1, :] * math.exp(-0.5 * m * m)
        )
        total = term if total is None else total + term
    return total


def near_kernel(
    distances_ref,
    mask_ref,
    filter_ref,
    own_ref,
    near_ref,
    far_tiles_ref,
    tiles_ref,
    *,
    step,
    part=32,
):
    rows = distances_ref.shape[0]
    radial_count = filter_ref.shape[0]
    middle = radial_count // 2
    sibling = 2 - 2 * lax.axis_index("waves")

    def make(low, block, put):
        start = block * rows if isinstance(block, int) else pl.multiple_of(block * rows, rows)
        d = distances_ref[low : low + part, pl.ds(start, rows)]
        mask = mask_ref[low : low + part, pl.ds(start, rows)].astype(jnp.float32)
        u = d * (0.5 / radius_cut)
        quarter = u * horner(sin_terms, u * u)
        half = 1.0 - 0.5**0.5 * quarter * quarter
        y = d * ((radial_count - 1) / radius_cut) - float(middle)
        centre = half * half * mask * jnp.exp(-0.5 * y * y)
        ratio = jnp.exp(y)
        back = jnp.exp(-y)
        put(middle, centre.astype(jnp.bfloat16))
        value = centre
        for k in range(middle + 1, radial_count):
            value = value * ratio
            put(k, value.astype(jnp.bfloat16))
        value = centre
        for k in range(middle - 1, -1, -1):
            value = value * back
            put(k, value.astype(jnp.bfloat16))

    block_values = own_ref[:rows, :]

    def products(i):
        found = jnp.dot(tiles_ref[i % 2], block_values, preferred_element_type=jnp.float32)
        near_ref[i * step : (i + 1) * step, :] = weighted(found, step, filter_ref)

    for i in range(rows // step):
        for low in range(i * step, (i + 1) * step, part):
            inner = low - i * step

            def put(k, value):
                at = k * step + inner
                tiles_ref[i % 2, at : at + part, :] = value

            def put_far(column):
                def store(k, value):
                    at = k * rows + low
                    far_tiles_ref[at : at + part, column : column + rows] = value

                return store

            make(low, 1, put)
            make(low, sibling, put_far(0))
            make(low, 2 - sibling, put_far(rows))
        if i:
            products(i - 1)
    products(rows // step - 1)


def near_masks(blocks):
    return sorted({a ^ ((a + 1) % blocks) for a in range(blocks)})


def pick_kernel(*refs):
    own_ref, chunks, out_ref = refs[0], refs[1:-1], refs[-1]
    rows = out_ref.shape[0] // 2
    out_ref[:rows, :] = own_ref[:rows, :]
    blocks, block = lax.axis_size("atoms"), lax.axis_index("atoms")
    side = lax.rem(block + 1 - 2 * lax.axis_index("waves") + blocks, blocks)
    for mask, chunk in zip(near_masks(blocks), chunks):

        @pl.when((block ^ side) == mask)
        def _():
            out_ref[rows:, :] = chunk[:rows, :]


def beyond_kernel(
    scale,
    near_in_ref,
    far_tiles_ref,
    filter_ref,
    side_ref,
    features_ref,
    turned_ref,
    shared_ref,
    combined_ref,
):
    rows = near_in_ref.shape[0]
    found = jnp.dot(far_tiles_ref[...], side_ref[...], preferred_element_type=jnp.float32)
    far = jnp.dot(turned_ref[...], shared_ref[...], preferred_element_type=jnp.float32)
    combined_ref[...] = (
        features_ref[...].astype(jnp.float32)
        + near_in_ref[...]
        + weighted(found, rows, filter_ref)
        + far * scale
    )


def update_kernel(
    scale,
    count_ref,
    combined_ref,
    received_ref,
    turned_ref,
    gain_ref,
    w_inner_ref,
    w_outer_ref,
    out_ref,
):
    quarter = received_ref.shape[0] // 4
    received = jnp.concatenate(
        [received_ref[i * quarter : (i + 1) * quarter, :] for i in (1, 0, 3, 2)], axis=0
    )
    far = jnp.dot(turned_ref[...], received, preferred_element_type=jnp.float32)
    combined = combined_ref[...] + far * scale
    spread = lax.rsqrt(jnp.mean(combined * combined, axis=-1, keepdims=True) + 1e-06)
    normed = (combined * spread * gain_ref[...]).astype(jnp.bfloat16)
    inner = jnp.dot(normed, w_inner_ref[...], preferred_element_type=jnp.float32)
    inner = (inner / (1.0 + jnp.exp(-inner))).astype(jnp.bfloat16)
    result = jnp.dot(inner, w_outer_ref[...], preferred_element_type=jnp.float32)
    row = lax.broadcasted_iota(jnp.int32, result.shape, 0)
    out_ref[...] = jnp.where(row < count_ref[:1, :1], result, 0.0).astype(jnp.bfloat16)


smem = pl.BlockSpec(memory_space=pltpu.SMEM)
vmem = pl.BlockSpec(memory_space=pltpu.VMEM)


def call(kernel, specs, outs, scratch=(), micros=1.0, mib=8, final=False):
    make = jax.ShapeDtypeStruct if final else pltpu.VMEM
    shapes = tuple(make(shape, dtype) for shape, dtype in outs)
    return pl.pallas_call(
        kernel,
        in_specs=specs,
        out_specs=tuple(vmem for _ in outs),
        out_shape=shapes,
        scratch_shapes=list(scratch),
        cost_estimate=pl.CostEstimate(
            flops=int(micros * 1.1e9), bytes_accessed=int(micros * 1e6), transcendentals=0
        ),
        compiler_params=pltpu.CompilerParams(vmem_limit_bytes=mib * 1024 * 1024),
    )


def gathered_parts(
    features,
    positions,
    distances,
    pair_mask,
    counts,
    wave_index,
    w_value,
    filter_short,
    filter_long,
    gain,
    w_inner,
    w_outer,
):
    rows, width = features.shape
    radial_count = filter_short.shape[0]
    wave_count = wave_index.shape[1]
    blocks, cores = lax.axis_size("atoms"), lax.axis_size("waves")
    bf16, f32 = jnp.bfloat16, jnp.float32

    def across(mask):
        return [
            (a * cores + c, (a ^ mask) * cores + c) for a in range(blocks) for c in range(cores)
        ]

    over = [(a * cores + c, a * cores + 1 - c) for a in range(blocks) for c in range(cores)]

    chunk_rows = rows + extra_rows
    (blank,) = call(blank_kernel, [], [((8, 128), jnp.int32)], micros=6.0)()
    counts, blank = lax.optimization_barrier((counts, blank))
    (held,) = call(count_kernel, [smem, vmem], [((8, 128), jnp.int32)])(counts, blank)
    (chunk,) = call(
        prepare_kernel, [vmem] * 4, [((chunk_rows, width), bf16)], micros=0.3
    )(held, features, w_value, positions)

    def move(value, mask):
        return lax.ppermute(value, both, across(mask))

    def swap(value):
        return lax.ppermute(value, both, over)

    starts, passed = move_masks(blocks)
    got = {0: chunk, **{mask: move(chunk, mask) for mask in starts}}
    for mask in passed:
        got[mask] = lax.ppermute(got[starts[0]], both, across(starts[0] ^ mask))
    other_waves = swap(wave_index)

    wave_total = wave_count * cores
    sums_shape = ((2 * wave_total, width), f32)
    waves, wave_weights = call(
        functools.partial(waves_kernel, float(rows * blocks * cores) ** -0.5),
        [vmem] * 3,
        [((wave_total, extra_rows), bf16), ((wave_total, width), f32)],
        micros=1.0,
    )(wave_index, other_waves, filter_long)
    step = rows // 4
    near, far_tiles = call(
        functools.partial(near_kernel, step=step),
        [vmem] * 4,
        [((rows, width), f32), ((radial_count * rows, 2 * rows), bf16)],
        [pltpu.VMEM((2, radial_count * step, rows), bf16)],
        micros=2.5,
        mib=16,
    )(distances, pair_mask, filter_short, chunk)

    first, *later, last = sum_groups(blocks)
    sums, turned = call(
        first_kernel,
        [vmem] * (1 + len(first)),
        [sums_shape, ((rows, 2 * wave_total), bf16)],
        [phase_scratch(len(first), rows, wave_total)],
        micros=0.9 * len(first),
        mib=12,
    )(waves, *(got[mask] for mask in first))
    (side,) = call(
        pick_kernel, [vmem] * (1 + len(near_masks(blocks))), [((2 * rows, width), bf16)], micros=0.3
    )(chunk, *(got[mask] for mask in near_masks(blocks)))
    side = swap(side)
    for masks in later:
        (sums,) = call(
            more_kernel,
            [vmem] * (2 + len(masks)),
            [sums_shape],
            [phase_scratch(len(masks), rows, wave_total)],
            micros=0.9 * len(masks),
            mib=12,
        )(waves, sums, *(got[mask] for mask in masks))
    (shared,) = call(
        last_kernel,
        [vmem] * (3 + len(last)),
        [(sums_shape[0], bf16)],
        [phase_scratch(len(last), rows, wave_total), pltpu.VMEM(sums_shape[0], f32)],
        micros=0.9 * len(last),
        mib=12,
    )(waves, sums, wave_weights, *(got[mask] for mask in last))
    received = swap(shared)
    scale = float(wave_total) ** -0.5
    (combined,) = call(
        functools.partial(beyond_kernel, scale),
        [vmem] * 7,
        [((rows, width), f32)],
        micros=1.5,
        mib=12,
    )(near, far_tiles, filter_short, side, features, turned, shared)
    return call(
        functools.partial(update_kernel, scale),
        [vmem] * 7,
        [((rows, width), bf16)],
        micros=1.0,
        final=True,
    )(held, combined, received, turned, jnp.reshape(gain, (1, width)), w_inner, w_outer)[0]


def phase_scratch(chunks, rows, waves, blocks=2):
    return pltpu.VMEM((blocks, 2 * waves // blocks, chunks * rows), jnp.bfloat16)


def gathered_body(*args):
    return gathered_parts(*args)


def move_masks(blocks):
    half = blocks // 2
    direct = list(range(half - 1, 0, -1))
    return [half] + direct, [half ^ mask for mask in direct]


def sum_groups(blocks):
    starts, passed = move_masks(blocks)
    groups = [[0] + starts[-1:] + starts[:1], starts[1:-1], passed[:1], passed[1:]]
    return [group for group in groups if group]


def gathers(mesh):
    blocks, cores = mesh.shape["atoms"], mesh.shape["waves"]
    return cores == 2 and 4 <= blocks <= gather_limit and blocks & (blocks - 1) == 0


def solution(mesh):
    placed = (
        P(("groups", "atoms", "waves"), None),
        P(None, ("groups", "atoms", "waves")),
        P(("groups", "atoms", "waves"), None),
        P(("groups", "atoms", "waves"), None),
        P(("groups", "atoms", "waves")),
        P(None, ("groups", "waves")),
        P(),
        P(),
        P(),
        P(),
        P(),
        P(),
    )
    mapped = jax.shard_map(
        gathered_body if gathers(mesh) else summed_body,
        mesh=mesh,
        in_specs=placed,
        out_specs=P(("groups", "atoms", "waves"), None),
        check_vma=False,
    )
    return mapped if gathers(mesh) else mapped
```

```python
import functools
import math

import jax
import jax.numpy as jnp
from jax import lax
from jax.experimental import pallas as pl
from jax.experimental.pallas import tpu as pltpu
from jax.sharding import PartitionSpec as P

radius_cut = 5.0
wave_top = 6.0 * 3.0**0.5
both = ("atoms", "waves")
gather_limit = 8
extra_rows = 16

sin_terms = (2.641737538071335, -1.0859062893731768, 0.13047468843565363)


def padded(block, sides, width):
    for axis, dim in sides:
        count = lax.axis_size(axis)
        forward = [(i, i + 1) for i in range(count - 1)]
        forward.append((count - 1, 0))
        backward = [(target, source) for source, target in forward]
        low = lax.ppermute(
            lax.slice_in_dim(block, block.shape[dim] - width, None, axis=dim), axis, forward
        )
        high = lax.ppermute(lax.slice_in_dim(block, 0, width, axis=dim), axis, backward)
        block = jnp.concatenate([low, block, high], axis=dim)
    return block


def radial_tiles(distances, pair_mask, radial_count):
    centres = radius_cut * jnp.arange(radial_count, dtype=jnp.float32) / (radial_count - 1)
    spacing = radius_cut / (radial_count - 1)
    envelope = (
        0.5 * (jnp.cos(jnp.pi * distances / radius_cut) + 1.0) * pair_mask.astype(jnp.float32)
    )
    offsets = (distances[None] - centres[:, None, None]) / spacing
    tiles = jnp.exp(-0.5 * offsets * offsets) * envelope[None]
    return tiles.astype(jnp.bfloat16)


def phase_tiles(points, wave_index):
    waves = wave_index.astype(jnp.float32)
    theta = points[0][:, None] * waves[0][None, :] + points[1][:, None] * waves[1][None, :]
    theta = 2.0 * jnp.pi * (theta + points[2][:, None] * waves[2][None, :])
    return (jnp.cos(theta).astype(jnp.bfloat16), jnp.sin(theta).astype(jnp.bfloat16))


def wave_filter(wave_index, filter_long):
    waves = wave_index.astype(jnp.float32)
    radial_count = filter_long.shape[0]
    magnitude = jnp.sqrt(waves[0] * waves[0] + waves[1] * waves[1] + waves[2] * waves[2])
    centres = wave_top * jnp.arange(radial_count, dtype=jnp.float32) / (radial_count - 1)
    spacing = wave_top / (radial_count - 1)
    offsets = (magnitude[None, :] - centres[:, None]) / spacing
    k_basis = jnp.exp(-0.5 * offsets * offsets)
    return jnp.dot(k_basis.T, filter_long, precision=lax.Precision.HIGHEST)


def summed_body(
    features,
    positions,
    distances,
    pair_mask,
    counts,
    wave_index,
    w_value,
    filter_short,
    filter_long,
    gain,
    w_inner,
    w_outer,
):
    row_count = features.shape[0]
    width = features.shape[1]
    radial_count = filter_short.shape[0]
    occupied = (lax.iota(jnp.int32, row_count) < counts[0]).astype(jnp.float32)
    values = (
        jnp.dot(features, w_value, preferred_element_type=jnp.float32) * occupied[:, None]
    ).astype(jnp.bfloat16)
    beside_all = padded(values, ((("atoms", "waves"), 0),), row_count)
    tiles = radial_tiles(distances, pair_mask, radial_count).reshape(
        radial_count * row_count, 3 * row_count
    )
    products = jnp.dot(tiles, beside_all, preferred_element_type=jnp.float32).reshape(
        radial_count, row_count, width
    )
    near_field = jnp.sum(products * filter_short[:, None, :], axis=0)
    wide_values, block_points = (
        lax.all_gather(values.astype(jnp.float32), "waves", axis=0, tiled=True),
        lax.all_gather(positions, "waves", axis=1, tiled=True),
    )
    block_values = wide_values.astype(jnp.bfloat16)
    cosine, sine = phase_tiles(block_points, wave_index)
    cos_sum = jnp.einsum("ak,af->kf", cosine, block_values, preferred_element_type=jnp.float32)
    sin_sum = jnp.einsum("ak,af->kf", sine, block_values, preferred_element_type=jnp.float32)
    atom_total = row_count * lax.axis_size(("atoms", "waves"))
    wave_total = wave_index.shape[1] * lax.axis_size("waves")
    factor_scale = float(atom_total) ** (-0.5)
    cos_total, sin_total = lax.psum((cos_sum, sin_sum), "atoms")
    block_filter = wave_filter(wave_index, filter_long)
    cos_filtered = (cos_total * block_filter * factor_scale).astype(jnp.bfloat16)
    sin_filtered = (sin_total * block_filter * factor_scale).astype(jnp.bfloat16)
    far_field = lax.psum_scatter(
        (
            jnp.dot(cosine, cos_filtered, preferred_element_type=jnp.float32)
            + jnp.dot(sine, sin_filtered, preferred_element_type=jnp.float32)
        ).astype(jnp.bfloat16),
        "waves",
        scatter_dimension=0,
        tiled=True,
    ).astype(jnp.float32) * float(wave_total) ** (-0.5)
    combined = features.astype(jnp.float32) + near_field + far_field
    normed = (
        combined * lax.rsqrt(jnp.mean(combined * combined, axis=-1, keepdims=True) + 1e-06) * gain
    ).astype(jnp.bfloat16)
    inner = jax.nn.silu(jnp.dot(normed, w_inner, preferred_element_type=jnp.float32)).astype(
        jnp.bfloat16
    )
    result = jnp.dot(inner, w_outer, preferred_element_type=jnp.float32) * occupied[:, None]
    return result.astype(jnp.bfloat16)


def horner(terms, w):
    total = jnp.full_like(w, terms[-1])
    for term in terms[-2::-1]:
        total = total * w + term
    return total


def phases(turns):
    r = turns - jnp.round(turns)
    quarter = r * horner(sin_terms, r * r)
    square = quarter * quarter
    rest = 2.0**1.5 - square
    half_sin = quarter * (rest * lax.rsqrt(rest))
    half_cos = 2.0**0.5 - square
    return 1.0 - half_sin * half_sin, half_sin * half_cos


def add_sums(sums_in, sums_ref, chunks, wave_ref, phase_ref, turned_ref=None, step=64):
    rows = chunks[0].shape[0] - extra_rows
    wave_count = wave_ref.shape[0]
    block = wave_count // phase_ref.shape[0]
    block_values = [chunk[:rows, :] for chunk in chunks]
    block_values = jnp.concatenate(block_values, axis=0) if len(chunks) > 1 else block_values[0]
    for index, start in enumerate(range(0, wave_count, block)):
        slot = phase_ref.at[index]
        for i, chunk in enumerate(chunks):
            part = slice(i * rows, (i + 1) * rows)
            for low in range(0, block, step):
                turns = jnp.dot(
                    wave_ref[start + low : start + low + step, :],
                    chunk[rows:, :],
                    preferred_element_type=jnp.float32,
                )
                cosine, sine = phases(turns)
                slot[low : low + step, part] = cosine.astype(jnp.bfloat16)
                slot[block + low : block + low + step, part] = sine.astype(jnp.bfloat16)
        found = jnp.dot(slot[...], block_values, preferred_element_type=jnp.float32)
        for first, rank in ((start, 0), (wave_count + start, block)):
            value = found[rank : rank + block, :]
            if sums_in is not None:
                value = sums_in[first : first + block, :] + value
            sums_ref[first : first + block, :] = value
            if turned_ref is not None:
                turned_ref[:, first : first + block] = slot[rank : rank + block, :rows].T


def pieces(value):
    high = value.astype(jnp.bfloat16).astype(jnp.float32)
    middle = (value - high).astype(jnp.bfloat16).astype(jnp.float32)
    return high, middle, value - high - middle


def blank_kernel(blank_ref):
    blank_ref[...] = jnp.zeros(blank_ref.shape, blank_ref.dtype)


def count_kernel(count_ref, blank_ref, held_ref):
    held_ref[...] = blank_ref[...] + count_ref[0]


def prepare_kernel(count_ref, features, w_value, positions, chunk_ref):
    rows = features.shape[0]
    values = jnp.dot(features[...], w_value[...], preferred_element_type=jnp.float32)
    row = lax.broadcasted_iota(jnp.int32, values.shape, 0)
    chunk_ref[:rows, :] = jnp.where(row < count_ref[:1, :1], values, 0.0).astype(jnp.bfloat16)
    points = positions[...]
    high, middle, low = pieces(points)
    spare = jnp.zeros((extra_rows - 9, rows), jnp.float32)
    chunk_ref[rows:, :] = jnp.concatenate([high, middle, low, spare], axis=0).astype(jnp.bfloat16)


def waves_kernel(
    scale, own_wave_ref, other_wave_ref, filter_long_ref, waves_ref, weights_ref
):
    waves = jnp.concatenate([own_wave_ref[...], other_wave_ref[...]], axis=1).astype(jnp.float32)
    spare = jnp.zeros((extra_rows - 9, waves.shape[1]), jnp.float32)
    waves_ref[...] = jnp.concatenate([waves, waves, waves, spare], axis=0).T.astype(jnp.bfloat16)
    radial_count = filter_long_ref.shape[0]
    magnitude = jnp.sqrt(
        waves[0:1] * waves[0:1] + waves[1:2] * waves[1:2] + waves[2:3] * waves[2:3]
    )
    spacing = wave_top / (radial_count - 1)
    index = lax.broadcasted_iota(jnp.int32, (radial_count, waves.shape[1]), 0)
    offsets = magnitude / spacing - index.astype(jnp.float32)
    basis = jnp.exp(-0.5 * offsets * offsets)
    high, middle, low = pieces(basis)
    rows = jnp.concatenate([high, high, middle, high, low, middle], axis=0)
    high, middle, low = pieces(filter_long_ref[...])
    columns = jnp.concatenate([high, middle, high, low, high, middle], axis=0)
    weights_ref[...] = scale * jnp.dot(
        rows.T.astype(jnp.bfloat16),
        columns.astype(jnp.bfloat16),
        preferred_element_type=jnp.float32,
    )


def first_kernel(wave_ref, *refs):
    chunks, (sums_ref, turned_ref, phase_ref) = refs[:-3], refs[-3:]
    add_sums(None, sums_ref, chunks, wave_ref, phase_ref, turned_ref)


def more_kernel(wave_ref, sums_in_ref, *refs):
    chunks, (sums_ref, phase_ref) = refs[:-2], refs[-2:]
    add_sums(sums_in_ref, sums_ref, chunks, wave_ref, phase_ref)


def last_kernel(half, wave_ref, sums_in_ref, weights_ref, *refs):
    chunks, (shared_ref, phase_ref, sums_ref) = refs[:-3], refs[-3:]
    block = shared_ref.shape[0] // 2
    waves = wave_ref.at[half * block : (half + 1) * block]
    add_sums(None, sums_ref, chunks, waves, phase_ref)
    for rank in range(2):
        part = slice(rank * block, (rank + 1) * block)
        first = (2 * rank + half) * block
        total = sums_in_ref[first : first + block, :] + sums_ref[part, :]
        weights = weights_ref[half * block : (half + 1) * block, :]
        shared_ref[part, :] = (total * weights).astype(jnp.bfloat16)


def weighted(products, rows, filter_ref):
    radial_count = filter_ref.shape[0]
    total = None
    for k in range(radial_count):
        m = k - radial_count // 2
        term = products[k * rows : (k + 1) * rows, :] * (
            filter_ref[k : k + 1, :] * math.exp(-0.5 * m * m)
        )
        total = term if total is None else total + term
    return total


def near_kernel(
    distances_ref,
    mask_ref,
    filter_ref,
    own_ref,
    near_ref,
    far_tiles_ref,
    tiles_ref,
    *,
    step,
    part=32,
):
    rows = distances_ref.shape[0]
    radial_count = filter_ref.shape[0]
    middle = radial_count // 2
    sibling = 2 - 2 * lax.axis_index("waves")

    def make(low, block, put):
        start = block * rows if isinstance(block, int) else pl.multiple_of(block * rows, rows)
        d = distances_ref[low : low + part, pl.ds(start, rows)]
        mask = mask_ref[low : low + part, pl.ds(start, rows)].astype(jnp.float32)
        u = d * (0.5 / radius_cut)
        quarter = u * horner(sin_terms, u * u)
        half = 1.0 - 0.5**0.5 * quarter * quarter
        y = d * ((radial_count - 1) / radius_cut) - float(middle)
        centre = half * half * mask * jnp.exp(-0.5 * y * y)
        ratio = jnp.exp(y)
        back = jnp.exp(-y)
        put(middle, centre.astype(jnp.bfloat16))
        value = centre
        for k in range(middle + 1, radial_count):
            value = value * ratio
            put(k, value.astype(jnp.bfloat16))
        value = centre
        for k in range(middle - 1, -1, -1):
            value = value * back
            put(k, value.astype(jnp.bfloat16))

    block_values = own_ref[:rows, :]

    def products(i):
        found = jnp.dot(tiles_ref[i % 2], block_values, preferred_element_type=jnp.float32)
        near_ref[i * step : (i + 1) * step, :] = weighted(found, step, filter_ref)

    for i in range(rows // step):
        for low in range(i * step, (i + 1) * step, part):
            inner = low - i * step

            def put(k, value):
                at = k * step + inner
                tiles_ref[i % 2, at : at + part, :] = value

            def put_far(column):
                def store(k, value):
                    at = k * rows + low
                    far_tiles_ref[at : at + part, column : column + rows] = value

                return store

            make(low, 1, put)
            make(low, sibling, put_far(0))
            make(low, 2 - sibling, put_far(rows))
        if i:
            products(i - 1)
    products(rows // step - 1)


def near_masks(blocks):
    return sorted({a ^ ((a + 1) % blocks) for a in range(blocks)})


def pick_kernel(*refs):
    own_ref, chunks, out_ref = refs[0], refs[1:-1], refs[-1]
    rows = out_ref.shape[0] // 2
    out_ref[:rows, :] = own_ref[:rows, :]
    blocks, block = lax.axis_size("atoms"), lax.axis_index("atoms")
    side = lax.rem(block + 1 - 2 * lax.axis_index("waves") + blocks, blocks)
    for mask, chunk in zip(near_masks(blocks), chunks):

        @pl.when((block ^ side) == mask)
        def _():
            out_ref[rows:, :] = chunk[:rows, :]


def joined(mine_ref, others_ref):
    block = mine_ref.shape[0] // 2
    parts = [ref[i * block : (i + 1) * block, :] for i in range(2) for ref in (mine_ref, others_ref)]
    return jnp.concatenate(parts, axis=0)


def beyond_kernel(
    scale,
    near_in_ref,
    far_tiles_ref,
    filter_ref,
    side_ref,
    features_ref,
    turned_ref,
    mine_ref,
    others_ref,
    combined_ref,
):
    rows = near_in_ref.shape[0]
    found = jnp.dot(far_tiles_ref[...], side_ref[...], preferred_element_type=jnp.float32)
    shared = joined(mine_ref, others_ref)
    far = jnp.dot(turned_ref[...], shared, preferred_element_type=jnp.float32)
    combined_ref[...] = (
        features_ref[...].astype(jnp.float32)
        + near_in_ref[...]
        + weighted(found, rows, filter_ref)
        + far * scale
    )


def update_kernel(
    scale,
    count_ref,
    combined_ref,
    mine_ref,
    others_ref,
    turned_ref,
    gain_ref,
    w_inner_ref,
    w_outer_ref,
    out_ref,
):
    received = joined(mine_ref, others_ref)
    far = jnp.dot(turned_ref[...], received, preferred_element_type=jnp.float32)
    combined = combined_ref[...] + far * scale
    spread = lax.rsqrt(jnp.mean(combined * combined, axis=-1, keepdims=True) + 1e-06)
    normed = (combined * spread * gain_ref[...]).astype(jnp.bfloat16)
    inner = jnp.dot(normed, w_inner_ref[...], preferred_element_type=jnp.float32)
    inner = (inner / (1.0 + jnp.exp(-inner))).astype(jnp.bfloat16)
    result = jnp.dot(inner, w_outer_ref[...], preferred_element_type=jnp.float32)
    row = lax.broadcasted_iota(jnp.int32, result.shape, 0)
    out_ref[...] = jnp.where(row < count_ref[:1, :1], result, 0.0).astype(jnp.bfloat16)


smem = pl.BlockSpec(memory_space=pltpu.SMEM)
vmem = pl.BlockSpec(memory_space=pltpu.VMEM)


def call(kernel, specs, outs, scratch=(), micros=1.0, mib=8, final=False):
    make = jax.ShapeDtypeStruct if final else pltpu.VMEM
    shapes = tuple(make(shape, dtype) for shape, dtype in outs)
    return pl.pallas_call(
        kernel,
        in_specs=specs,
        out_specs=tuple(vmem for _ in outs),
        out_shape=shapes,
        scratch_shapes=list(scratch),
        cost_estimate=pl.CostEstimate(
            flops=int(micros * 1.1e9), bytes_accessed=int(micros * 1e6), transcendentals=0
        ),
        compiler_params=pltpu.CompilerParams(vmem_limit_bytes=mib * 1024 * 1024),
    )


def gathered_parts(
    features,
    positions,
    distances,
    pair_mask,
    counts,
    wave_index,
    w_value,
    filter_short,
    filter_long,
    gain,
    w_inner,
    w_outer,
):
    rows, width = features.shape
    radial_count = filter_short.shape[0]
    wave_count = wave_index.shape[1]
    blocks, cores = lax.axis_size("atoms"), lax.axis_size("waves")
    bf16, f32 = jnp.bfloat16, jnp.float32

    def across(mask):
        return [
            (a * cores + c, (a ^ mask) * cores + c) for a in range(blocks) for c in range(cores)
        ]

    over = [(a * cores + c, a * cores + 1 - c) for a in range(blocks) for c in range(cores)]

    chunk_rows = rows + extra_rows
    (blank,) = call(blank_kernel, [], [((8, 128), jnp.int32)], micros=6.0)()
    counts, blank = lax.optimization_barrier((counts, blank))
    (held,) = call(count_kernel, [smem, vmem], [((8, 128), jnp.int32)])(counts, blank)
    (chunk,) = call(
        prepare_kernel, [vmem] * 4, [((chunk_rows, width), bf16)], micros=0.3
    )(held, features, w_value, positions)

    def move(value, mask):
        return lax.ppermute(value, both, across(mask))

    def swap(value):
        return lax.ppermute(value, both, over)

    starts, passed = move_masks(blocks)
    got = {0: chunk, **{mask: move(chunk, mask) for mask in starts}}
    for mask in passed:
        got[mask] = lax.ppermute(got[starts[0]], both, across(starts[0] ^ mask))
    other_waves = swap(wave_index)

    wave_total = wave_count * cores
    sums_shape = ((2 * wave_total, width), f32)
    waves, wave_weights = call(
        functools.partial(waves_kernel, float(rows * blocks * cores) ** -0.5),
        [vmem] * 3,
        [((wave_total, extra_rows), bf16), ((wave_total, width), f32)],
        micros=1.0,
    )(wave_index, other_waves, filter_long)
    step = rows // 4
    near, far_tiles = call(
        functools.partial(near_kernel, step=step),
        [vmem] * 4,
        [((rows, width), f32), ((radial_count * rows, 2 * rows), bf16)],
        [pltpu.VMEM((2, radial_count * step, rows), bf16)],
        micros=2.5,
        mib=16,
    )(distances, pair_mask, filter_short, chunk)

    first, *later, last = sum_groups(blocks)
    sums, turned = call(
        first_kernel,
        [vmem] * (1 + len(first)),
        [sums_shape, ((rows, 2 * wave_total), bf16)],
        [phase_scratch(len(first), rows, wave_total)],
        micros=0.9 * len(first),
        mib=12,
    )(waves, *(got[mask] for mask in first))
    (side,) = call(
        pick_kernel, [vmem] * (1 + len(near_masks(blocks))), [((2 * rows, width), bf16)], micros=0.3
    )(chunk, *(got[mask] for mask in near_masks(blocks)))
    side = swap(side)
    for masks in later:
        (sums,) = call(
            more_kernel,
            [vmem] * (2 + len(masks)),
            [sums_shape],
            [phase_scratch(len(masks), rows, wave_total)],
            micros=0.9 * len(masks),
            mib=12,
        )(waves, sums, *(got[mask] for mask in masks))
    shared, received = [], []
    half_shape = (sums_shape[0][0] // 2, width)
    for half in range(2):
        shared += call(
            functools.partial(last_kernel, half),
            [vmem] * (3 + len(last)),
            [(half_shape, bf16)],
            [phase_scratch(len(last), rows, wave_total // 2), pltpu.VMEM(half_shape, f32)],
            micros=0.5 * len(last),
            mib=12,
        )(waves, sums, wave_weights, *(got[mask] for mask in last))
        received.append(swap(shared[half]))
    scale = float(wave_total) ** -0.5
    (combined,) = call(
        functools.partial(beyond_kernel, scale),
        [vmem] * 8,
        [((rows, width), f32)],
        micros=1.5,
        mib=12,
    )(near, far_tiles, filter_short, side, features, turned, *shared)
    return call(
        functools.partial(update_kernel, scale),
        [vmem] * 8,
        [((rows, width), bf16)],
        micros=1.0,
        final=True,
    )(held, combined, *received[::-1], turned, jnp.reshape(gain, (1, width)), w_inner, w_outer)[0]


def phase_scratch(chunks, rows, waves, blocks=2):
    return pltpu.VMEM((blocks, 2 * waves // blocks, chunks * rows), jnp.bfloat16)


def gathered_body(*args):
    return gathered_parts(*args)


def move_masks(blocks):
    half = blocks // 2
    direct = list(range(half - 1, 0, -1))
    return [half] + direct, [half ^ mask for mask in direct]


def sum_groups(blocks):
    starts, passed = move_masks(blocks)
    groups = [[0] + starts[-1:] + starts[:1], starts[1:-1], passed[:1], passed[1:]]
    return [group for group in groups if group]


def gathers(mesh):
    blocks, cores = mesh.shape["atoms"], mesh.shape["waves"]
    return cores == 2 and 4 <= blocks <= gather_limit and blocks & (blocks - 1) == 0


def solution(mesh):
    placed = (
        P(("groups", "atoms", "waves"), None),
        P(None, ("groups", "atoms", "waves")),
        P(("groups", "atoms", "waves"), None),
        P(("groups", "atoms", "waves"), None),
        P(("groups", "atoms", "waves")),
        P(None, ("groups", "waves")),
        P(),
        P(),
        P(),
        P(),
        P(),
        P(),
    )
    mapped = jax.shard_map(
        gathered_body if gathers(mesh) else summed_body,
        mesh=mesh,
        in_specs=placed,
        out_specs=P(("groups", "atoms", "waves"), None),
        check_vma=False,
    )
    return mapped if gathers(mesh) else mapped
```
